32 devices in a mesh: row: 4 (over z), col: 8 (over y, x, core).
Axes of the slice: x: 2, y: 2, z: 4, core: 2. Of those that a mesh axis runs over, the one named last changes fastest.
Arguments:
- frontal: float32 [4096, 16384], P('row', 'col'), may hold values from -6 to 6
- sketch: float32 [16384, 256], P('col'), may hold values from -0.046875 to 0.046875
- rank_table: int32 [3, 4], replicated, may hold values from 64 to 256, as said below
Outputs:
- leaf_basis: float32 [4096, 256], P(('row', 'col'))
- top_basis: float32 [4096, 256], P(('row', 'col'))
- coupling: float32 [1024, 16384], P('row', 'col')
The draws below stay inside these ranges and needn't reach their ends.
Inputs may be any that keep to these rules, and one draw needn't show every extreme that they name: rank_table[l, g] is the rank of the level-l node made of the 2**l consecutive row groups holding g, equal over the groups of that node; a node's rank is at most the larger of its two children's ranks; in every draw some leaf has rank 256 and some leaf rank 256 // 4.
All inputs are finite; a program needn't handle non-finite values.
Results may differ from the reference program's by a relative error of at most 0.00012.
Values sent between devices are 32-bit elements; how exact they have to be, the bound alone decides.
No kernel may reach another device: no remote copies, remote signals or barrier semaphores. Data moves between devices by JAX's collectives and lax.ppermute only.
A program may use at most 64 MiB of HBM per device.

```python
import jax
import jax.numpy as jnp
from jax import lax

S = 256
LEVELS = 2
ROWS = 4096
COLS = 16384
N_ROW = 4


def draw_rank_table(key, part):
    lowest = S // 4
    leaf_key = jax.random.fold_in(key, 11)
    perm_key = jax.random.fold_in(key, 23)
    leaves = jax.random.randint(leaf_key, (N_ROW,), lowest, S + 1)
    order = jax.random.permutation(perm_key, N_ROW)
    leaves = leaves.at[order[0]].set(S)
    leaves = leaves.at[order[1]].set(lowest)
    leaves = leaves.astype(jnp.int32)
    rows_list = [leaves]
    previous = leaves
    for height in range(1, LEVELS + 1):
        node_span = 2 ** height
        child_ranks = previous.reshape(N_ROW // node_span, 2, node_span // 2)[:, :, 0]
        largest = jnp.max(child_ranks, axis=1)
        node_key = jax.random.fold_in(key, 100 + height)
        spread = jax.random.randint(node_key, (N_ROW // node_span,), 0, largest - lowest + 1)
        node_ranks = (lowest + spread).astype(jnp.int32)
        previous = jnp.repeat(node_ranks, node_span)
        rows_list.append(previous)
    return jnp.stack(rows_list, axis=0).astype(jnp.int32)


def strengthened(values, stream_key, source, target, shards_of, factor):
    def block_of(dim):
        return (jnp.arange(values.shape[dim]) // (values.shape[dim] // shards_of)).reshape((-1,) + (1,) * (values.ndim - 1 - dim))

    one_side = jax.random.permutation(stream_key, shards_of)[block_of(target)]
    second = (block_of(target) + shards_of // 2) % shards_of
    return jnp.where((block_of(source) == one_side) | (block_of(source) == second), factor * values, values)


def block_levels(stream_key, extent, pieces, least, top_value):
    loudness = 1.0
    for axis_at, shards_of in pieces:
        draws = jax.random.uniform(jax.random.fold_in(jax.random.fold_in(stream_key, 6), axis_at), (shards_of,), jnp.float32, least / len(pieces), top_value / len(pieces))
        loudness = loudness * jnp.repeat(jnp.exp(draws), extent[axis_at] // shards_of).reshape((-1,) + (1,) * (len(extent) - 1 - axis_at))
    return loudness


def normal_values(rng, extent, deviation, limit, split=(), kind=jnp.bfloat16):
    factor_of = block_levels(rng, extent, split, -0.22, 0.18) if split else 1.0
    drawn = jax.random.normal(rng, extent, jnp.float32) * deviation * factor_of
    return jnp.minimum(jnp.maximum(drawn, -limit), limit).astype(kind)


def heavy_noise(key, dims, scale, most, cuts, heavy, held_as=jnp.bfloat16):
    values = scale * jax.random.normal(key, dims, jnp.float32)
    if cuts:
        values = values * block_levels(key, dims, cuts, -0.22, 0.18)
    return jnp.clip(strengthened(values, jax.random.fold_in(key, 3), *heavy), -most, most).astype(held_as)


def setup_inputs(seed: int = 0) -> dict:
    key_of = jax.random.split(jax.random.key(seed), 4)
    return {
        "frontal": heavy_noise(key_of[0], (ROWS, COLS), 1.0, 6.0, ((0, 4), (1, 8)), (1, 0, 8, 2.0), jnp.float32),
        "sketch": normal_values(key_of[1], (COLS, S), COLS ** -0.5, 0.046875, ((0, 8),), jnp.float32),
        "rank_table": draw_rank_table(jax.random.fold_in(key_of[3], 71), 0),
    }


def product(left, right):
    return jnp.dot(left.astype(jnp.float32), right.astype(jnp.float32), precision=lax.Precision.HIGHEST, preferred_element_type=jnp.float32)

def mask_of(rank_value, width):
    return (jnp.arange(width) < rank_value).astype(jnp.float32)

def factor(gram_full, keep_mask):
    masked = keep_mask[:, None] * gram_full * keep_mask[None, :] + jnp.diag(1.0 - keep_mask)
    return jnp.linalg.cholesky(masked)

def right_solve(factor_low, operand):
    return lax.linalg.triangular_solve(factor_low, operand, left_side=False, lower=True, transpose_a=True)

def left_solve(factor_low, operand):
    return lax.linalg.triangular_solve(factor_low, operand, left_side=True, lower=True)

def reference(frontal, sketch, rank_table):
    width = sketch.shape[1]
    groups = rank_table.shape[1]
    row_count = frontal.shape[0] // groups
    bases = []
    coords = []
    couplings = []
    for member in range(groups):
        row_block = frontal[member * row_count:(member + 1) * row_count]
        samples = product(row_block, sketch)
        gram_full = product(samples.T, samples)
        keep_mask = mask_of(rank_table[0, member], width)
        factor_low = factor(gram_full, keep_mask)
        leaf_basis = right_solve(factor_low, samples * keep_mask[None, :])
        bases.append(leaf_basis)
        coords.append(left_solve(factor_low, keep_mask[:, None] * gram_full))
        couplings.append(product(leaf_basis.T, row_block))
    chains = [jnp.eye(width, dtype=jnp.float32) for member in range(groups)]
    for height in range(1, LEVELS + 1):
        node_span = 2 ** height
        half_span = node_span // 2
        for first_group in range(0, groups, node_span):
            coords_low = coords[first_group]
            coords_high = coords[first_group + half_span]
            pair_gram = product(coords_low.T, coords_low) + product(coords_high.T, coords_high)
            node_mask = mask_of(rank_table[height, first_group], width)
            factor_low = factor(pair_gram, node_mask)
            transfer_low = right_solve(factor_low, coords_low * node_mask[None, :])
            transfer_high = right_solve(factor_low, coords_high * node_mask[None, :])
            parent_coords = left_solve(factor_low, node_mask[:, None] * pair_gram)
            for member in range(first_group, first_group + node_span):
                if member < first_group + half_span:
                    chains[member] = product(chains[member], transfer_low)
                else:
                    chains[member] = product(chains[member], transfer_high)
                coords[member] = parent_coords
    leaf_basis = jnp.concatenate(bases, axis=0)
    top_basis = jnp.concatenate([product(bases[member], chains[member]) for member in range(groups)], axis=0)
    coupling = jnp.concatenate(couplings, axis=0)
    return (leaf_basis, top_basis, coupling)
```

```python
import functools

import jax
import jax.numpy as jnp
from jax import lax
from jax.experimental import pallas as pl
from jax.experimental.pallas import tpu as pltpu
from jax.sharding import PartitionSpec as P

LEVELS = 2
TILE = 8
BLOCK = 64
F32 = jnp.float32
BF16 = jnp.bfloat16
EXACT = lax.Precision.HIGHEST
VMEM = pl.BlockSpec(memory_space=pltpu.VMEM)
SMEM = pl.BlockSpec(memory_space=pltpu.SMEM)


def contract(left, right, dim_left, dim_right, precision=None):
    return lax.dot_general(
        left, right, (((dim_left,), (dim_right,)), ((), ())), precision=precision, preferred_element_type=F32
    )


def halves(value):
    high = value.astype(BF16)
    return high, (value - high.astype(F32)).astype(BF16)


def contract3(left, right, dim_left, dim_right):
    (lh, ll), (rh, rl) = left, right
    return (
        contract(lh, rh, dim_left, dim_right)
        + contract(lh, rl, dim_left, dim_right)
        + contract(ll, rh, dim_left, dim_right)
    )


def eye_like(shape):
    rows = lax.broadcasted_iota(jnp.int32, shape, 0)
    cols = lax.broadcasted_iota(jnp.int32, shape, 1)
    return (rows == cols).astype(F32)


def over_lanes(tile, lane):
    return jnp.broadcast_to(tile[:, lane : lane + 1], tile.shape)


def over_rows(tile, row):
    return jnp.broadcast_to(tile[row : row + 1, :], tile.shape)


def small_inverse_factor(block):
    n = block.shape[0]
    wide = jnp.concatenate([block, eye_like((n, n))], axis=1)
    work = [wide[TILE * t : TILE * (t + 1)] for t in range(n // TILE)]
    row_of = lax.broadcasted_iota(jnp.int32, work[0].shape, 0)
    out = []
    for t in range(len(work)):
        cols = {u: [over_lanes(work[u], TILE * t + k) for k in range(TILE)] for u in range(t, len(work))}
        pivots = None
        for j in range(TILE):
            across = [over_rows(cols[t][k], j) if k >= j else None for k in range(TILE)]
            pivot = across[j]
            scale = 1.0 / pivot
            pivot_row = over_rows(work[t], j)
            pivots = pivot if pivots is None else jnp.where(row_of == j, pivot, pivots)
            for u in range(t, len(work)):
                step = cols[u][j] * scale
                if u == t:
                    step = jnp.where(row_of > j, step, 0.0)
                for k in range(j + 1, TILE):
                    cols[u][k] = cols[u][k] - step * across[k]
                work[u] = work[u] - step * pivot_row
        out.append(work[t] * lax.rsqrt(pivots))
    return jnp.concatenate(out, axis=0)[:, n:]


def masked_inverse_factor(gram, rank, s_ref, p_ref):
    n = gram.shape[0]
    rows = lax.broadcasted_iota(jnp.int32, (n, n), 0)
    cols = lax.broadcasted_iota(jnp.int32, (n, n), 1)
    s_ref[...] = jnp.where((rows < rank) & (cols < rank), gram, (rows == cols).astype(F32))
    p_ref[...] = (rows == cols).astype(F32)
    for low in range(0, n, BLOCK):
        high = low + BLOCK
        inverse = small_inverse_factor(s_ref[low:high, low:high])
        extra = contract(inverse, p_ref[low:high, :], 1, 0, EXACT)
        p_ref[low:high, :] = extra
        if high < n:
            panel = contract(inverse, s_ref[low:high, :], 1, 0, EXACT)
            s_ref[high:, :] = s_ref[high:, :] - contract(panel[:, high:], panel, 0, 0, EXACT)
            p_ref[high:, :] = p_ref[high:, :] - contract(panel[:, high:], extra, 0, 0, EXACT)
    p_ref[...] = jnp.where(rows < rank, p_ref[...], 0.0)


def samples_kernel(index_ref, frontal_ref, sketch_ref, out_ref, high_ref, low_ref):
    @pl.when(pl.program_id(0) == 0)
    def _():
        high_ref[...], low_ref[...] = halves(sketch_ref[...])

    out_ref[...] = contract3(halves(frontal_ref[...]), (high_ref[...], low_ref[...]), 1, 0)


def partial_samples(index, frontal, sketch, parts, offset):
    share = frontal.shape[0] // parts
    inner, width = sketch.shape
    return pl.pallas_call(
        samples_kernel,
        grid_spec=pltpu.PrefetchScalarGridSpec(
            num_scalar_prefetch=1,
            grid=(parts // 2,),
            in_specs=[
                pl.BlockSpec((share, inner), lambda d, index: (index[0] ^ (2 * d + offset), 0)),
                pl.BlockSpec((inner, width), lambda d, index: (0, 0)),
            ],
            out_specs=pl.BlockSpec((share, width), lambda d, index: (d, 0)),
            scratch_shapes=[pltpu.VMEM((inner, width), BF16)] * 2,
        ),
        out_shape=jax.ShapeDtypeStruct((frontal.shape[0] // 2, width), F32),
        name="partial_samples",
    )(index, frontal, sketch)


def leaf_kernel(rank_ref, *refs):
    pieces, (p_ref, coords_ref, own_ref, s_ref) = refs[:-4], refs[-4:]
    gram = None
    for piece in pieces:
        part = halves(piece[...])
        term = contract3(part, part, 0, 0)
        gram = term if gram is None else gram + term
    masked_inverse_factor(gram, rank_ref[0], s_ref, p_ref)
    coords = contract(p_ref[...], gram, 1, 0, EXACT)
    coords_ref[...] = coords
    own_ref[...] = contract(coords, coords, 0, 0, EXACT)


def leaf_factor(rank, pieces):
    width = pieces[0].shape[1]
    square = jax.ShapeDtypeStruct((width, width), F32)
    return pl.pallas_call(
        leaf_kernel,
        in_specs=[SMEM] + [VMEM] * len(pieces),
        out_specs=(VMEM,) * 3,
        out_shape=(square,) * 3,
        scratch_shapes=[pltpu.VMEM((width, width), F32)],
        name="leaf_factor",
    )(rank, *pieces)


def coupling_kernel(count, index_ref, p_ref, frontal_ref, *refs):
    pieces, (share_ref, out_ref, high_ref, low_ref) = refs[:count], refs[count:]
    share = pieces[0].shape[0]

    @pl.when(pl.program_id(0) == 0)
    def _():
        inverse = halves(p_ref[...])
        for at, piece in enumerate(pieces):
            basis = contract3(halves(piece[...]), inverse, 1, 1)
            if at == 0:
                share_ref[...] = basis
            start = pl.multiple_of((index_ref[0] ^ at) * share, share)
            high_ref[pl.ds(start, share), :], low_ref[pl.ds(start, share), :] = halves(basis)

    out_ref[...] = contract3((high_ref[...], low_ref[...]), halves(frontal_ref[...]), 0, 0)


def couplings(index, inverse, frontal, pieces, blocks=4):
    rows, cols = frontal.shape
    share, width = pieces[0].shape
    return pl.pallas_call(
        functools.partial(coupling_kernel, len(pieces)),
        grid_spec=pltpu.PrefetchScalarGridSpec(
            num_scalar_prefetch=1,
            grid=(blocks,),
            in_specs=[
                pl.BlockSpec((width, width), lambda b, index: (0, 0)),
                pl.BlockSpec((rows, cols // blocks), lambda b, index: (0, b)),
            ]
            + [pl.BlockSpec((share, width), lambda b, index: (0, 0))] * len(pieces),
            out_specs=(
                pl.BlockSpec((share, width), lambda b, index: (0, 0)),
                pl.BlockSpec((width, cols // blocks), lambda b, index: (0, b)),
            ),
            scratch_shapes=[pltpu.VMEM((rows, width), BF16)] * 2,
        ),
        out_shape=(jax.ShapeDtypeStruct((share, width), F32), jax.ShapeDtypeStruct((width, cols), F32)),
        name="couplings",
    )(index, inverse, frontal, *pieces)


def node_kernel(rank_ref, own_ref, sibling_ref, coords_ref, top_ref, next_own_ref, next_coords_ref, next_top_ref, s_ref, p_ref):
    pair = own_ref[...] + sibling_ref[...]
    masked_inverse_factor(pair, rank_ref[0], s_ref, p_ref)
    inverse = p_ref[...]
    upper = contract(inverse, pair, 1, 0, EXACT)
    next_coords_ref[...] = upper
    next_own_ref[...] = contract(upper, upper, 0, 0, EXACT)
    carried = contract(top_ref[...], coords_ref[...], 1, 0, EXACT)
    next_top_ref[...] = contract(carried, inverse, 1, 1, EXACT)


def node(rank, own, sibling, coords, top):
    width = own.shape[0]
    square = jax.ShapeDtypeStruct((width, width), F32)
    return pl.pallas_call(
        node_kernel,
        in_specs=[SMEM] + [VMEM] * 4,
        out_specs=(VMEM,) * 3,
        out_shape=(square, square, jax.ShapeDtypeStruct(top.shape, F32)),
        scratch_shapes=[pltpu.VMEM((width, width), F32)] * 2,
        name="node",
    )(rank, own, sibling, coords, top)


def swapped(block, axis, distance):
    count = lax.axis_size(axis)
    route = [(low, low ^ distance) for low in range(count) if low ^ distance < count]
    return lax.ppermute(block, axis, route)


def body(frontal, sketch, rank_table):
    parts = lax.axis_size("col")
    chips = parts // 2
    share = frontal.shape[0] // parts
    row_group = lax.axis_index("row")
    index = lax.axis_index("col").astype(jnp.int32).reshape(1)
    ranks = lax.dynamic_slice_in_dim(rank_table, row_group, 1, 1)

    leaving = partial_samples(index, frontal, sketch, parts, 1)
    arriving = swapped(leaving, "col", 1)
    staying = partial_samples(index, frontal, sketch, parts, 0)
    chip_sum = staying + arriving
    part_of = lambda at: chip_sum[at * share : (at + 1) * share]
    total = part_of(0)
    for other in [swapped(part_of(at), "col", 2 * at) for at in range(1, chips)]:
        total = total + other
    gathered = [total] + [swapped(total, "col", 2 * at) for at in range(1, chips)]
    pieces = []
    for piece in gathered:
        pieces += [piece, swapped(piece, "col", 1)]

    inverse, coords, own = leaf_factor(ranks[0], pieces)
    sibling = swapped(own, "row", 1)
    leaf_share, coupling = couplings(index, inverse, frontal, pieces)
    top = leaf_share
    for height in range(1, LEVELS + 1):
        if height > 1:
            sibling = swapped(own, "row", 1 << (height - 1))
        own, coords, top = node(ranks[height], own, sibling, coords, top)
    return (leaf_share, top, coupling)


def solution(mesh):
    return jax.shard_map(
        body,
        mesh=mesh,
        in_specs=(P("row", "col"), P("col", None), P()),
        out_specs=(P(("row", "col"), None), P(("row", "col"), None), P("row", "col")),
        check_vma=False,
    )
```

```python
import functools

import jax
import jax.numpy as jnp
from jax import lax
from jax.experimental import pallas as pl
from jax.experimental.pallas import tpu as pltpu
from jax.sharding import PartitionSpec as P

LEVELS = 2
TILE = 8
BLOCK = 64
LANES = 128
F32 = jnp.float32
BF16 = jnp.bfloat16
EXACT = lax.Precision.HIGHEST
VMEM = pl.BlockSpec(memory_space=pltpu.VMEM)
SMEM = pl.BlockSpec(memory_space=pltpu.SMEM)


def contract(left, right, dim_left, dim_right, precision=None):
    return lax.dot_general(
        left, right, (((dim_left,), (dim_right,)), ((), ())), precision=precision, preferred_element_type=F32
    )


def halves(value):
    high = value.astype(BF16)
    return high, (value - high.astype(F32)).astype(BF16)


def contract3(left, right, dim_left, dim_right):
    (lh, ll), (rh, rl) = left, right
    return (
        contract(lh, rh, dim_left, dim_right)
        + contract(lh, rl, dim_left, dim_right)
        + contract(ll, rh, dim_left, dim_right)
    )


def over_lanes(tile, lane):
    return jnp.broadcast_to(tile[:, lane : lane + 1], tile.shape)


def over_rows(tile, row):
    return jnp.broadcast_to(tile[row : row + 1, :], tile.shape)


def along_lanes(tile, index):
    return jnp.take_along_axis(tile, index, axis=1, mode="promise_in_bounds")


def eliminate(rows, rank, at):
    count = len(rows)
    sub = lax.broadcasted_iota(jnp.int32, (TILE, LANES), 0)
    lane = lax.broadcasted_iota(jnp.int32, (TILE, LANES), 1)
    inside = (lane >= at) & (lane < at + BLOCK)
    work = []
    for t in range(count):
        unit = (lane == sub + (TILE * t + BLOCK - at)).astype(F32)
        work.append([jnp.where(inside, rows[t][0], unit)] + list(rows[t][1:]))
    out = []
    diag = [over_lanes(work[0][0], at + k) for k in range(TILE)]
    for t in range(count):
        ahead = None
        if t + 1 < count:
            ahead = [over_lanes(work[t + 1][0], at + TILE * (t + 1) + k) for k in range(TILE)]
        pivots = None
        for j in range(TILE):
            below = [over_rows(diag[k], j) if k >= j else None for k in range(TILE)]
            pivot = below[j]
            scale = jnp.where(rank > TILE * t + j, 1.0 / pivot, 0.0)
            pivots = pivot if pivots is None else jnp.where(sub == j, pivot, pivots)
            row = [over_rows(part, j) for part in work[t]]
            scaled = [part * scale for part in row]
            step = jnp.where(sub > j, diag[j] * scale, 0.0)
            for k in range(j + 1, TILE):
                diag[k] = diag[k] - step * below[k]
            for u in range(t + 1, count):
                column = along_lanes(row[0], sub + (at + TILE * u))
                if u == t + 1:
                    column_scaled = column * scale
                    for k in range(TILE):
                        ahead[k] = ahead[k] - column_scaled * over_rows(column, k)
                work[u] = [part - column * other for part, other in zip(work[u], scaled)]
            work[t] = [part - step * other for part, other in zip(work[t], row)]
        root = jnp.where(sub + TILE * t < rank, lax.rsqrt(pivots), 0.0)
        out.append([part * root for part in work[t]])
        diag = ahead
    return out


def masked_factor(s_ref, rank, coords_ref, p_ref, own_ref=None):
    n = s_ref.shape[0]
    row_of = lax.broadcasted_iota(jnp.int32, (BLOCK, n), 0)
    col_of = lax.broadcasted_iota(jnp.int32, (BLOCK, n), 1)
    p_ref[...] = jnp.zeros((n, n), F32)
    if own_ref is not None:
        own_ref[...] = jnp.zeros((n, n), F32)
    for low in range(0, n, BLOCK):
        high = low + BLOCK
        slab = low // LANES * LANES
        at = low - slab
        starts = [slab] + ([slab] if at + BLOCK < LANES else []) + list(range(slab + LANES, n, LANES))
        rows = [[s_ref[r : r + TILE, c : c + LANES] for c in starts] for r in range(low, high, TILE)]
        out = eliminate(rows, rank - low, at)
        main = jnp.concatenate([tiles[0] for tiles in out], axis=0)
        inverse = main[:, BLOCK - at : 2 * BLOCK - at]
        slabs = {c: jnp.concatenate([tiles[q] for tiles in out], axis=0) for q, c in enumerate(starts)}
        panel = jnp.concatenate([slabs[c] for c in range(slab, n, LANES)], axis=1)
        panel = jnp.where(col_of[:, slab:] >= row_of[:, slab:] + low, panel, 0.0)
        if coords_ref is not None:
            if slab:
                coords_ref[low:high, :slab] = jnp.zeros((BLOCK, slab), F32)
            coords_ref[low:high, slab:] = panel
        split = halves(panel)
        if high < n or own_ref is not None:
            gram = contract3(split, split, 0, 0)
            if own_ref is not None:
                own_ref[slab:, slab:] = own_ref[slab:, slab:] + gram
            if high < n:
                s_ref[high:, slab:] = s_ref[high:, slab:] - gram[high - slab :, :]
        if low:
            p_ref[low:high, :] = contract3(halves(inverse), halves(p_ref[low:high, :]), 1, 0)
        if at:
            inverse = jnp.concatenate([jnp.zeros((BLOCK, at), F32), inverse], axis=1)
            p_ref[low:high, slab:high] = p_ref[low:high, slab:high] + inverse
        else:
            p_ref[low:high, low:high] = inverse
        if high < n:
            right = tuple(part[:, high - slab :] for part in split)
            p_ref[high:, :] = p_ref[high:, :] - contract3(right, halves(p_ref[low:high, :]), 0, 0)


def samples_kernel(index_ref, frontal_ref, sketch_ref, out_ref, high_ref, low_ref):
    @pl.when(pl.program_id(0) == 0)
    def _():
        high_ref[...], low_ref[...] = halves(sketch_ref[...])

    out_ref[...] = contract3(halves(frontal_ref[...]), (high_ref[...], low_ref[...]), 1, 0)


def partial_samples(index, frontal, sketch, parts, offset):
    share = frontal.shape[0] // parts
    inner, width = sketch.shape
    return pl.pallas_call(
        samples_kernel,
        grid_spec=pltpu.PrefetchScalarGridSpec(
            num_scalar_prefetch=1,
            grid=(parts // 2,),
            in_specs=[
                pl.BlockSpec((share, inner), lambda d, index: (index[0] ^ (2 * d + offset), 0)),
                pl.BlockSpec((inner, width), lambda d, index: (0, 0)),
            ],
            out_specs=pl.BlockSpec((share, width), lambda d, index: (d, 0)),
            scratch_shapes=[pltpu.VMEM((inner, width), BF16)] * 2,
        ),
        out_shape=jax.ShapeDtypeStruct((frontal.shape[0] // 2, width), F32),
        name="partial_samples",
    )(index, frontal, sketch)


def leaf_kernel(rank_ref, *refs):
    pieces, (p_ref, coords_ref, own_ref, s_ref) = refs[:-4], refs[-4:]
    samples = halves(jnp.concatenate([piece[...] for piece in pieces], axis=0))
    s_ref[...] = contract3(samples, samples, 0, 0)
    masked_factor(s_ref, rank_ref[0], coords_ref, p_ref, own_ref)


def leaf_factor(rank, pieces):
    width = pieces[0].shape[1]
    square = jax.ShapeDtypeStruct((width, width), F32)
    return pl.pallas_call(
        leaf_kernel,
        in_specs=[SMEM] + [VMEM] * len(pieces),
        out_specs=(VMEM,) * 3,
        out_shape=(square,) * 3,
        scratch_shapes=[pltpu.VMEM((width, width), F32)],
        name="leaf_factor",
    )(rank, *pieces)


def coupling_kernel(count, index_ref, p_ref, frontal_ref, *refs):
    pieces, (share_ref, out_ref, high_ref, low_ref) = refs[:count], refs[count:]
    share = pieces[0].shape[0]

    @pl.when(pl.program_id(0) == 0)
    def _():
        inverse = halves(p_ref[...])
        for at, piece in enumerate(pieces):
            basis = contract3(halves(piece[...]), inverse, 1, 1)
            if at == 0:
                share_ref[...] = basis
            start = pl.multiple_of((index_ref[0] ^ at) * share, share)
            high_ref[pl.ds(start, share), :], low_ref[pl.ds(start, share), :] = halves(basis)

    out_ref[...] = contract3((high_ref[...], low_ref[...]), halves(frontal_ref[...]), 0, 0)


def couplings(index, inverse, frontal, pieces, blocks=4):
    rows, cols = frontal.shape
    share, width = pieces[0].shape
    return pl.pallas_call(
        functools.partial(coupling_kernel, len(pieces)),
        grid_spec=pltpu.PrefetchScalarGridSpec(
            num_scalar_prefetch=1,
            grid=(blocks,),
            in_specs=[
                pl.BlockSpec((width, width), lambda b, index: (0, 0)),
                pl.BlockSpec((rows, cols // blocks), lambda b, index: (0, b)),
            ]
            + [pl.BlockSpec((share, width), lambda b, index: (0, 0))] * len(pieces),
            out_specs=(
                pl.BlockSpec((share, width), lambda b, index: (0, 0)),
                pl.BlockSpec((width, cols // blocks), lambda b, index: (0, b)),
            ),
            scratch_shapes=[pltpu.VMEM((rows, width), BF16)] * 2,
        ),
        out_shape=(jax.ShapeDtypeStruct((share, width), F32), jax.ShapeDtypeStruct((width, cols), F32)),
        name="couplings",
    )(index, inverse, frontal, *pieces)


def carried_top(top_ref, coords_ref):
    return halves(contract3(halves(top_ref[...]), halves(coords_ref[...]), 1, 0))


def node_kernel(rank_ref, own_ref, sibling_ref, coords_ref, top_ref, next_own_ref, next_coords_ref, next_top_ref, s_ref, p_ref):
    s_ref[...] = own_ref[...] + sibling_ref[...]
    carried = carried_top(top_ref, coords_ref)
    masked_factor(s_ref, rank_ref[0], next_coords_ref, p_ref, next_own_ref)
    next_top_ref[...] = contract3(carried, halves(p_ref[...]), 1, 1)


def last_node_kernel(rank_ref, own_ref, sibling_ref, coords_ref, top_ref, next_top_ref, s_ref, p_ref):
    s_ref[...] = own_ref[...] + sibling_ref[...]
    carried = carried_top(top_ref, coords_ref)
    masked_factor(s_ref, rank_ref[0], None, p_ref)
    next_top_ref[...] = contract3(carried, halves(p_ref[...]), 1, 1)


def node(rank, own, sibling, coords, top, last):
    width = own.shape[0]
    square = jax.ShapeDtypeStruct((width, width), F32)
    out_shape = (square,) * (0 if last else 2) + (jax.ShapeDtypeStruct(top.shape, F32),)
    return pl.pallas_call(
        last_node_kernel if last else node_kernel,
        in_specs=[SMEM] + [VMEM] * 4,
        out_specs=(VMEM,) * len(out_shape),
        out_shape=out_shape,
        scratch_shapes=[pltpu.VMEM((width, width), F32)] * 2,
        name="last_node" if last else "node",
    )(rank, own, sibling, coords, top)


def swapped(block, axis, distance):
    count = lax.axis_size(axis)
    route = [(low, low ^ distance) for low in range(count) if low ^ distance < count]
    return lax.ppermute(block, axis, route)


def body(frontal, sketch, rank_table):
    parts = lax.axis_size("col")
    chips = parts // 2
    share = frontal.shape[0] // parts
    row_group = lax.axis_index("row")
    index = lax.axis_index("col").astype(jnp.int32).reshape(1)
    ranks = lax.dynamic_slice_in_dim(rank_table, row_group, 1, 1)

    leaving = partial_samples(index, frontal, sketch, parts, 1)
    arriving = swapped(leaving, "col", 1)
    staying = partial_samples(index, frontal, sketch, parts, 0)
    chip_sum = staying + arriving
    part_of = lambda at: chip_sum[at * share : (at + 1) * share]
    total = part_of(0)
    for other in [swapped(part_of(at), "col", 2 * at) for at in range(1, chips)]:
        total = total + other
    gathered = [total] + [swapped(total, "col", 2 * at) for at in range(1, chips)]
    pieces = []
    for piece in gathered:
        pieces += [piece, swapped(piece, "col", 1)]

    inverse, coords, own = leaf_factor(ranks[0], pieces)
    sibling = swapped(own, "row", 1)
    leaf_share, coupling = couplings(index, inverse, frontal, pieces)
    top = leaf_share
    for height in range(1, LEVELS):
        own, coords, top = node(ranks[height], own, sibling, coords, top, False)
        sibling = swapped(own, "row", 1 << height)
    (top,) = node(ranks[LEVELS], own, sibling, coords, top, True)
    return (leaf_share, top, coupling)


def solution(mesh):
    return jax.shard_map(
        body,
        mesh=mesh,
        in_specs=(P("row", "col"), P("col", None), P()),
        out_specs=(P(("row", "col"), None), P(("row", "col"), None), P("row", "col")),
        check_vma=False,
    )
```

```python
import functools

import jax
import jax.numpy as jnp
from jax import lax
from jax.experimental import pallas as pl
from jax.experimental.pallas import tpu as pltpu
from jax.sharding import PartitionSpec as P

LEVELS = 2
TILE = 8
GROUP = 16
LANES = 128
F32 = jnp.float32
BF16 = jnp.bfloat16
EXACT = lax.Precision.HIGHEST
VMEM = pl.BlockSpec(memory_space=pltpu.VMEM)
SMEM = pl.BlockSpec(memory_space=pltpu.SMEM)


def contract(left, right, dim_left, dim_right, precision=None):
    return lax.dot_general(
        left, right, (((dim_left,), (dim_right,)), ((), ())), precision=precision, preferred_element_type=F32
    )


def halves(value):
    high = value.astype(BF16)
    return high, (value - high.astype(F32)).astype(BF16)


def contract3(left, right, dim_left, dim_right):
    (lh, ll), (rh, rl) = left, right
    return (
        contract(lh, rh, dim_left, dim_right)
        + contract(lh, rl, dim_left, dim_right)
        + contract(ll, rh, dim_left, dim_right)
    )


def over_lanes(tile, lane):
    return jnp.broadcast_to(tile[:, lane : lane + 1], tile.shape)


def over_rows(tile, row):
    return jnp.broadcast_to(tile[row : row + 1, :], tile.shape)


def along_lanes(tile, index):
    return jnp.take_along_axis(tile, index, axis=1, mode="promise_in_bounds")


def packed_contract3(left, right):
    (lh, ll), (rh, rl) = left, right
    return contract(jnp.concatenate([lh, lh, ll], axis=0), jnp.concatenate([rh, rl, rh], axis=0), 0, 0)


def eliminate(parts, outs, low, rank, update):
    n = parts[0][0].shape[0]
    at = low - parts[0][1]
    own = GROUP // TILE
    count = min(2 * own, (n - low) // TILE)
    sub = lax.broadcasted_iota(jnp.int32, (TILE, LANES), 0)
    lane = lax.broadcasted_iota(jnp.int32, (TILE, LANES), 1)
    span = lambda t: slice(low + TILE * t, low + TILE * (t + 1))
    work = [[ref[span(t), c : c + LANES] for ref, c in parts] for t in range(count)]
    less = update()
    diag = [over_lanes(work[0][0], at + k) for k in range(TILE)]
    for t in range(own):
        left = rank - (low + TILE * t)
        for k in range(TILE):
            diag[k] = jnp.where((sub < left) & (left > k), diag[k], (sub == k).astype(F32))
        pivots = None
        for j in range(TILE):
            below = [over_rows(diag[k], j) if k >= j else None for k in range(TILE)]
            pivot = below[j]
            scale = 1.0 / pivot
            lower = jnp.where(sub > j, diag[j], 0.0)
            for k in range(j + 1, TILE):
                diag[k] = diag[k] - (lower * below[k]) * scale
            pivots = pivot if pivots is None else jnp.where(sub == j, pivot, pivots)
            scale = jnp.where(left > j, scale, 0.0)
            row = [over_rows(part, j) for part in work[t]]
            scaled = [part * scale for part in row]
            for u in range(t + 1, count):
                ahead_of = at + TILE * u
                column = along_lanes(row[ahead_of // LANES], sub + ahead_of % LANES)
                work[u] = [part - column * other for part, other in zip(work[u], scaled)]
            work[t] = [part - lower * other for part, other in zip(work[t], scaled)]
        root = jnp.where(sub < left, lax.rsqrt(pivots), 0.0)
        for part, (ref, c, upper) in zip(work[t], outs):
            part = part * root
            if upper:
                part = jnp.where(lane + c >= sub + (low + TILE * t), part, 0.0)
            ref[span(t), c : c + LANES] = part
        if t + 1 < own:
            diag = [over_lanes(work[t + 1][0], at + TILE * (t + 1) + k) for k in range(TILE)]
    past = low + GROUP
    for t in range(own, count):
        for q, (ref, c) in enumerate(parts):
            part = work[t][q]
            if less is not None and less[q] is not None:
                part = part - less[q][TILE * (t - own) : TILE * (t - own + 1)]
            ref[span(t), c : c + LANES] = part
    if less is not None:
        for q, (ref, c) in enumerate(parts):
            if less[q] is not None and low + TILE * count < n:
                ref[low + TILE * count :, c : c + LANES] = (
                    ref[low + TILE * count :, c : c + LANES] - less[q][TILE * (count - own) :]
                )


def masked_factor(s_ref, e_ref, rank, coords_ref, x_ref, own_ref=None, growing=False):
    n = s_ref.shape[0]
    wide = e_ref.shape[1]
    coords_ref[...] = jnp.zeros(coords_ref.shape, F32)
    x_ref[...] = jnp.zeros(x_ref.shape, F32)
    if own_ref is not None:
        own_ref[...] = s_ref[...]
    extent_at = lambda low: min(wide, low // LANES * LANES + LANES) if growing else wide
    for low in range(0, n, GROUP):
        slab = low // LANES * LANES
        s_at = list(range(slab, n, LANES))
        e_at = list(range(0, extent_at(low), LANES))
        parts = [(s_ref, c) for c in s_at] + [(e_ref, c) for c in e_at]
        outs = [(coords_ref, c, True) for c in s_at] + [(x_ref, c, False) for c in e_at]

        def update(low=low, slab=slab, s_at=s_at, e_at=e_at):
            past = low + GROUP
            if low == 0 or past >= n:
                return None
            before = slice(low - GROUP, low)
            panel = halves(coords_ref[before, slab:])
            known = extent_at(low - GROUP)
            right = panel
            if known:
                right = tuple(
                    jnp.concatenate(pair, axis=1) for pair in zip(panel, halves(x_ref[before, :known]))
                )
            product = packed_contract3(tuple(part[:, past - slab :] for part in panel), right)
            less = [product[:, c - slab : c - slab + LANES] for c in s_at]
            return less + [
                product[:, n - slab + c : n - slab + c + LANES] if c < known else None for c in e_at
            ]

        pl.when(rank > low)(functools.partial(eliminate, parts, outs, low, rank, update))
    if own_ref is not None:

        @pl.when(rank < n)
        def _():
            rows = lax.broadcasted_iota(jnp.int32, (n, n), 0)
            cols = lax.broadcasted_iota(jnp.int32, (n, n), 1)
            panel = halves(coords_ref[...])
            outside = (rows < rank) | (cols < rank)
            own_ref[...] = jnp.where(outside, own_ref[...], contract3(panel, panel, 0, 0))


def samples_kernel(index_ref, frontal_ref, sketch_ref, out_ref, high_ref, low_ref):
    @pl.when(pl.program_id(0) == 0)
    def _():
        high_ref[...], low_ref[...] = halves(sketch_ref[...])

    out_ref[...] = contract3(halves(frontal_ref[...]), (high_ref[...], low_ref[...]), 1, 0)


def partial_samples(index, frontal, sketch, parts, offset):
    share = frontal.shape[0] // parts
    inner, width = sketch.shape
    return pl.pallas_call(
        samples_kernel,
        grid_spec=pltpu.PrefetchScalarGridSpec(
            num_scalar_prefetch=1,
            grid=(parts // 2,),
            in_specs=[
                pl.BlockSpec((share, inner), lambda d, index: (index[0] ^ (2 * d + offset), 0)),
                pl.BlockSpec((inner, width), lambda d, index: (0, 0)),
            ],
            out_specs=pl.BlockSpec((share, width), lambda d, index: (d, 0)),
            scratch_shapes=[pltpu.VMEM((inner, width), BF16)] * 2,
        ),
        out_shape=jax.ShapeDtypeStruct((frontal.shape[0] // 2, width), F32),
        name="partial_samples",
    )(index, frontal, sketch)


def unit_matrix(shape):
    rows = lax.broadcasted_iota(jnp.int32, shape, 0)
    cols = lax.broadcasted_iota(jnp.int32, shape, 1)
    return (rows == cols).astype(F32)


def leaf_kernel(rank_ref, *refs):
    pieces, (p_ref, coords_ref, own_ref, s_ref, e_ref) = refs[:-5], refs[-5:]
    e_ref[...] = unit_matrix(e_ref.shape)
    samples = halves(jnp.concatenate([piece[...] for piece in pieces], axis=0))
    s_ref[...] = contract3(samples, samples, 0, 0)
    masked_factor(s_ref, e_ref, rank_ref[0], coords_ref, p_ref, own_ref, growing=True)


def leaf_factor(rank, pieces):
    width = pieces[0].shape[1]
    square = jax.ShapeDtypeStruct((width, width), F32)
    return pl.pallas_call(
        leaf_kernel,
        in_specs=[SMEM] + [VMEM] * len(pieces),
        out_specs=(VMEM,) * 3,
        out_shape=(square,) * 3,
        scratch_shapes=[pltpu.VMEM((width, width), F32)] * 2,
        name="leaf_factor",
    )(rank, *pieces)


def coupling_kernel(count, index_ref, p_ref, frontal_ref, *refs):
    pieces, (share_ref, out_ref, high_ref, low_ref) = refs[:count], refs[count:]
    share = pieces[0].shape[0]

    @pl.when(pl.program_id(0) == 0)
    def _():
        inverse = halves(p_ref[...])
        for at, piece in enumerate(pieces):
            basis = contract3(halves(piece[...]), inverse, 1, 1)
            if at == 0:
                share_ref[...] = basis
            start = pl.multiple_of((index_ref[0] ^ at) * share, share)
            high_ref[pl.ds(start, share), :], low_ref[pl.ds(start, share), :] = halves(basis)

    out_ref[...] = contract3((high_ref[...], low_ref[...]), halves(frontal_ref[...]), 0, 0)


def couplings(index, inverse, frontal, pieces, blocks=4):
    rows, cols = frontal.shape
    share, width = pieces[0].shape
    return pl.pallas_call(
        functools.partial(coupling_kernel, len(pieces)),
        grid_spec=pltpu.PrefetchScalarGridSpec(
            num_scalar_prefetch=1,
            grid=(blocks,),
            in_specs=[
                pl.BlockSpec((width, width), lambda b, index: (0, 0)),
                pl.BlockSpec((rows, cols // blocks), lambda b, index: (0, b)),
            ]
            + [pl.BlockSpec((share, width), lambda b, index: (0, 0))] * len(pieces),
            out_specs=(
                pl.BlockSpec((share, width), lambda b, index: (0, 0)),
                pl.BlockSpec((width, cols // blocks), lambda b, index: (0, b)),
            ),
            scratch_shapes=[pltpu.VMEM((rows, width), BF16)] * 2,
        ),
        out_shape=(jax.ShapeDtypeStruct((share, width), F32), jax.ShapeDtypeStruct((width, cols), F32)),
        name="couplings",
    )(index, inverse, frontal, *pieces)


def node_start(first, own_ref, sibling_ref, coords_ref, top_ref, s_ref, e_ref):
    s_ref[...] = own_ref[...] + sibling_ref[...]
    carried = contract3(halves(coords_ref[...]), halves(top_ref[...]), 0, 1 if first else 0)
    if carried.shape[1] < e_ref.shape[1]:
        e_ref[...] = jnp.zeros(e_ref.shape, F32)
    e_ref[:, : carried.shape[1]] = carried


def node_kernel(first, rank_ref, own_ref, sibling_ref, coords_ref, top_ref, next_own_ref, next_coords_ref, next_top_ref, s_ref, e_ref):
    node_start(first, own_ref, sibling_ref, coords_ref, top_ref, s_ref, e_ref)
    masked_factor(s_ref, e_ref, rank_ref[0], next_coords_ref, next_top_ref, next_own_ref)


def last_node_kernel(first, rank_ref, own_ref, sibling_ref, coords_ref, top_ref, out_ref, s_ref, e_ref, r_ref, x_ref):
    node_start(first, own_ref, sibling_ref, coords_ref, top_ref, s_ref, e_ref)
    masked_factor(s_ref, e_ref, rank_ref[0], r_ref, x_ref)
    out_ref[...] = x_ref[...].T[: out_ref.shape[0], :]


def node(rank, own, sibling, coords, top, share, height):
    width = own.shape[0]
    padded = -(-share // LANES) * LANES
    square = jax.ShapeDtypeStruct((width, width), F32)
    scratch = [pltpu.VMEM((width, width), F32), pltpu.VMEM((width, padded), F32)]
    last = height == LEVELS
    if last:
        kernel, out_shape = last_node_kernel, (jax.ShapeDtypeStruct((share, width), F32),)
        scratch += scratch[:2]
    else:
        kernel, out_shape = node_kernel, (square, square, jax.ShapeDtypeStruct((width, padded), F32))
    return pl.pallas_call(
        functools.partial(kernel, height == 1),
        in_specs=[SMEM] + [VMEM] * 4,
        out_specs=(VMEM,) * len(out_shape),
        out_shape=out_shape,
        scratch_shapes=scratch,
        name="last_node" if last else "node",
    )(rank, own, sibling, coords, top)


def swapped(block, axis, distance):
    count = lax.axis_size(axis)
    route = [(low, low ^ distance) for low in range(count) if low ^ distance < count]
    return lax.ppermute(block, axis, route)


def body(frontal, sketch, rank_table):
    parts = lax.axis_size("col")
    chips = parts // 2
    share = frontal.shape[0] // parts
    row_group = lax.axis_index("row")
    index = lax.axis_index("col").astype(jnp.int32).reshape(1)
    ranks = lax.dynamic_slice_in_dim(rank_table, row_group, 1, 1)

    leaving = partial_samples(index, frontal, sketch, parts, 1)
    arriving = swapped(leaving, "col", 1)
    staying = partial_samples(index, frontal, sketch, parts, 0)
    chip_sum = staying + arriving
    part_of = lambda at: chip_sum[at * share : (at + 1) * share]
    total = part_of(0)
    for other in [swapped(part_of(at), "col", 2 * at) for at in range(1, chips)]:
        total = total + other
    gathered = [total] + [swapped(total, "col", 2 * at) for at in range(1, chips)]
    pieces = []
    for piece in gathered:
        pieces += [piece, swapped(piece, "col", 1)]

    inverse, coords, own = leaf_factor(ranks[0], pieces)
    sibling = swapped(own, "row", 1)
    leaf_share, coupling = couplings(index, inverse, frontal, pieces)
    top = leaf_share
    for height in range(1, LEVELS):
        own, coords, top = node(ranks[height], own, sibling, coords, top, share, height)
        sibling = swapped(own, "row", 1 << height)
    (top,) = node(ranks[LEVELS], own, sibling, coords, top, share, LEVELS)
    return (leaf_share, top, coupling)


def solution(mesh):
    return jax.shard_map(
        body,
        mesh=mesh,
        in_specs=(P("row", "col"), P("col", None), P()),
        out_specs=(P(("row", "col"), None), P(("row", "col"), None), P("row", "col")),
        check_vma=False,
    )
```

```python
import functools

import jax
import jax.numpy as jnp
from jax import lax
from jax.experimental import pallas as pl
from jax.experimental.pallas import tpu as pltpu
from jax.sharding import PartitionSpec as P

LEVELS = 2
TILE = 8
GROUP = 16
LANES = 128
F32 = jnp.float32
BF16 = jnp.bfloat16
EXACT = lax.Precision.HIGHEST
VMEM = pl.BlockSpec(memory_space=pltpu.VMEM)
SMEM = pl.BlockSpec(memory_space=pltpu.SMEM)


def contract(left, right, dim_left, dim_right, precision=None):
    return lax.dot_general(
        left, right, (((dim_left,), (dim_right,)), ((), ())), precision=precision, preferred_element_type=F32
    )


def halves(value):
    high = value.astype(BF16)
    return high, (value - high.astype(F32)).astype(BF16)


def contract3(left, right, dim_left, dim_right):
    (lh, ll), (rh, rl) = left, right
    return (
        contract(lh, rh, dim_left, dim_right)
        + contract(lh, rl, dim_left, dim_right)
        + contract(ll, rh, dim_left, dim_right)
    )


def over_lanes(tile, lane):
    return jnp.broadcast_to(tile[:, lane : lane + 1], tile.shape)


def over_rows(tile, row):
    return jnp.broadcast_to(tile[row : row + 1, :], tile.shape)


def along_lanes(tile, index):
    return jnp.take_along_axis(tile, index, axis=1, mode="promise_in_bounds")


def packed_contract3(left, right):
    (lh, ll), (rh, rl) = left, right
    return contract(jnp.concatenate([lh, lh, ll], axis=0), jnp.concatenate([rh, rl, rh], axis=0), 0, 0)


def eliminate(parts, outs, low, rank, update):
    n = parts[0][0].shape[0]
    at = low - parts[0][1]
    own = GROUP // TILE
    count = min(2 * own, (n - low) // TILE)
    sub = lax.broadcasted_iota(jnp.int32, (TILE, LANES), 0)
    lane = lax.broadcasted_iota(jnp.int32, (TILE, LANES), 1)
    span = lambda t: slice(low + TILE * t, low + TILE * (t + 1))
    work = [[ref[span(t), c : c + LANES] for ref, c in parts] for t in range(count)]
    less = update()
    diag = [over_lanes(work[0][0], at + k) for k in range(TILE)]
    for t in range(own):
        left = rank - (low + TILE * t)
        for k in range(TILE):
            diag[k] = jnp.where((sub < left) & (left > k), diag[k], (sub == k).astype(F32))
        pivots = None
        for j in range(TILE):
            below = [over_rows(diag[k], j) if k >= j else None for k in range(TILE)]
            pivot = below[j]
            scale = 1.0 / pivot
            lower = jnp.where(sub > j, diag[j], 0.0)
            for k in range(j + 1, TILE):
                diag[k] = diag[k] - (lower * below[k]) * scale
            pivots = pivot if pivots is None else jnp.where(sub == j, pivot, pivots)
            scale = jnp.where(left > j, scale, 0.0)
            row = [over_rows(part, j) for part in work[t]]
            scaled = [part * scale for part in row]
            for u in range(t + 1, count):
                ahead_of = at + TILE * u
                column = along_lanes(row[ahead_of // LANES], sub + ahead_of % LANES)
                work[u] = [part - column * other for part, other in zip(work[u], scaled)]
            work[t] = [part - lower * other for part, other in zip(work[t], scaled)]
        root = jnp.where(sub < left, lax.rsqrt(pivots), 0.0)
        for part, (ref, c, upper) in zip(work[t], outs):
            part = part * root
            if upper:
                part = jnp.where(lane + c >= sub + (low + TILE * t), part, 0.0)
            ref[span(t), c : c + LANES] = part
        if t + 1 < own:
            diag = [over_lanes(work[t + 1][0], at + TILE * (t + 1) + k) for k in range(TILE)]
    past = low + GROUP
    for t in range(own, count):
        for q, (ref, c) in enumerate(parts):
            part = work[t][q]
            if less is not None and less[q] is not None:
                part = part - less[q][TILE * (t - own) : TILE * (t - own + 1)]
            ref[span(t), c : c + LANES] = part
    if less is not None:
        for q, (ref, c) in enumerate(parts):
            if less[q] is not None and low + TILE * count < n:
                ref[low + TILE * count :, c : c + LANES] = (
                    ref[low + TILE * count :, c : c + LANES] - less[q][TILE * (count - own) :]
                )


def masked_factor(s_ref, e_ref, rank, coords_ref, x_ref, own_ref=None, growing=False):
    n = s_ref.shape[0]
    wide = e_ref.shape[1]
    coords_ref[...] = jnp.zeros(coords_ref.shape, F32)
    x_ref[...] = jnp.zeros(x_ref.shape, F32)
    if own_ref is not None:
        own_ref[...] = s_ref[...]
    extent_at = lambda low: min(wide, low // LANES * LANES + LANES) if growing else wide
    for low in range(0, n, GROUP):
        slab = low // LANES * LANES
        s_at = list(range(slab, n, LANES))
        e_at = list(range(0, extent_at(low), LANES))
        parts = [(s_ref, c) for c in s_at] + [(e_ref, c) for c in e_at]
        outs = [(coords_ref, c, True) for c in s_at] + [(x_ref, c, False) for c in e_at]

        def update(low=low, slab=slab, s_at=s_at, e_at=e_at):
            past = low + GROUP
            if low == 0 or past >= n:
                return None
            before = slice(low - GROUP, low)
            panel = halves(coords_ref[before, slab:])
            known = extent_at(low - GROUP)
            right = panel
            if known:
                right = tuple(
                    jnp.concatenate(pair, axis=1) for pair in zip(panel, halves(x_ref[before, :known]))
                )
            product = packed_contract3(tuple(part[:, past - slab :] for part in panel), right)
            less = [product[:, c - slab : c - slab + LANES] for c in s_at]
            return less + [
                product[:, n - slab + c : n - slab + c + LANES] if c < known else None for c in e_at
            ]

        pl.when(rank > low)(functools.partial(eliminate, parts, outs, low, rank, update))
    if own_ref is not None:

        @pl.when(rank < n)
        def _():
            rows = lax.broadcasted_iota(jnp.int32, (n, n), 0)
            cols = lax.broadcasted_iota(jnp.int32, (n, n), 1)
            panel = halves(coords_ref[...])
            outside = (rows < rank) | (cols < rank)
            own_ref[...] = jnp.where(outside, own_ref[...], contract3(panel, panel, 0, 0))


def samples_kernel(count, index_ref, *refs):
    frontal_refs, (sketch_ref, out_ref) = refs[:count], refs[count:]
    rows = halves(jnp.concatenate([ref[...] for ref in frontal_refs], axis=0))
    term = contract3(rows, halves(sketch_ref[...]), 1, 0)

    @pl.when(pl.program_id(0) == 0)
    def _():
        out_ref[...] = term

    @pl.when(pl.program_id(0) > 0)
    def _():
        out_ref[...] = out_ref[...] + term


def partial_samples(index, frontal, sketch, parts, offset, blocks=4):
    share = frontal.shape[0] // parts
    inner, width = sketch.shape
    step = inner // blocks
    count = parts // 2

    def rows_of(d):
        return pl.BlockSpec((share, step), lambda k, index: (index[0] ^ (2 * d + offset), k))

    return pl.pallas_call(
        functools.partial(samples_kernel, count),
        grid_spec=pltpu.PrefetchScalarGridSpec(
            num_scalar_prefetch=1,
            grid=(blocks,),
            in_specs=[rows_of(d) for d in range(count)] + [pl.BlockSpec((step, width), lambda k, index: (k, 0))],
            out_specs=pl.BlockSpec((count * share, width), lambda k, index: (0, 0)),
        ),
        out_shape=jax.ShapeDtypeStruct((count * share, width), F32),
        name="partial_samples",
    )(index, *[frontal] * count, sketch)


def unit_matrix(shape):
    rows = lax.broadcasted_iota(jnp.int32, shape, 0)
    cols = lax.broadcasted_iota(jnp.int32, shape, 1)
    return (rows == cols).astype(F32)


def pack_half(square_ref, half_ref, core):
    mid = square_ref.shape[0] // 2
    first = core == 0
    half_ref[:mid, :] = jnp.where(first, square_ref[:mid, :mid], square_ref[mid:, mid:])
    half_ref[mid:, :] = jnp.where(first, square_ref[: mid // 2, mid:], square_ref[mid // 2 : mid, mid:])


def leaf_kernel(rank_ref, core_ref, *refs):
    pieces, (p_ref, coords_ref, own_ref, half_ref, s_ref, e_ref) = refs[:-6], refs[-6:]
    e_ref[...] = unit_matrix(e_ref.shape)
    samples = halves(jnp.concatenate([piece[...] for piece in pieces], axis=0))
    s_ref[...] = contract3(samples, samples, 0, 0)
    masked_factor(s_ref, e_ref, rank_ref[0], coords_ref, p_ref, own_ref, growing=True)
    pack_half(own_ref, half_ref, core_ref[0])


def half_shape(width):
    return jax.ShapeDtypeStruct((width * 3 // 4, width // 2), F32)


def leaf_factor(rank, core, pieces):
    width = pieces[0].shape[1]
    square = jax.ShapeDtypeStruct((width, width), F32)
    return pl.pallas_call(
        leaf_kernel,
        in_specs=[SMEM] * 2 + [VMEM] * len(pieces),
        out_specs=(VMEM,) * 4,
        out_shape=(square,) * 3 + (half_shape(width),),
        scratch_shapes=[pltpu.VMEM((width, width), F32)] * 2,
        name="leaf_factor",
    )(rank, core, *pieces)


def first_coupling_kernel(count, index_ref, p_ref, frontal_ref, *refs):
    pieces, (share_ref, out_ref, high_ref, low_ref) = refs[:count], refs[count:]
    share = pieces[0].shape[0]

    @pl.when(pl.program_id(0) == 0)
    def _():
        inverse = halves(p_ref[...])
        for at, piece in enumerate(pieces):
            part = halves(piece[...])
            if at == 0:
                share_ref[...] = contract3(part, inverse, 1, 1)
            start = pl.multiple_of((index_ref[0] ^ at) * share, share)
            high, low = halves(contract3(part, inverse, 1, 1))
            high_ref[pl.ds(start, share), :] = high
            low_ref[pl.ds(start, share), :] = low

    out_ref[...] = contract3((high_ref[...], low_ref[...]), halves(frontal_ref[...]), 0, 0)


def first_couplings(index, inverse, frontal, pieces, blocks, done):
    rows, cols = frontal.shape
    share, width = pieces[0].shape
    split = jax.ShapeDtypeStruct((rows, width), BF16)
    whole = lambda shape: pl.BlockSpec(shape, lambda b, index: (0, 0))
    return pl.pallas_call(
        functools.partial(first_coupling_kernel, len(pieces)),
        grid_spec=pltpu.PrefetchScalarGridSpec(
            num_scalar_prefetch=1,
            grid=(done,),
            in_specs=[whole((width, width)), pl.BlockSpec((rows, cols // blocks), lambda b, index: (0, b))]
            + [whole((share, width))] * len(pieces),
            out_specs=(
                whole((share, width)),
                pl.BlockSpec((width, cols // blocks), lambda b, index: (0, b)),
                whole((rows, width)),
                whole((rows, width)),
            ),
        ),
        out_shape=(jax.ShapeDtypeStruct((share, width), F32), jax.ShapeDtypeStruct((width, cols), F32), split, split),
        name="first_couplings",
    )(index, inverse, frontal, *pieces)


def more_coupling_kernel(high_ref, low_ref, frontal_ref, before_ref, after_ref, out_ref):
    out_ref[...] = contract3((high_ref[...], low_ref[...]), halves(frontal_ref[...]), 0, 0)


def more_couplings(high, low, frontal, before, after, blocks, done):
    rows, cols = frontal.shape
    width = high.shape[1]
    whole = lambda shape: pl.BlockSpec(shape, lambda b: (0, 0))
    return pl.pallas_call(
        more_coupling_kernel,
        grid=(blocks - done,),
        in_specs=[
            whole((rows, width)),
            whole((rows, width)),
            pl.BlockSpec((rows, cols // blocks), lambda b: (0, b + done)),
            pl.BlockSpec(memory_space=pl.ANY),
            pl.BlockSpec(memory_space=pl.ANY),
        ],
        out_specs=pl.BlockSpec((width, cols // blocks), lambda b: (0, b + done)),
        out_shape=jax.ShapeDtypeStruct((width, cols), F32),
        input_output_aliases={3: 0},
        name="more_couplings",
    )(high, low, frontal, before, after)


def node_start(first, core, own_ref, half_refs, coords_ref, top_ref, s_ref, e_ref):
    mid = own_ref.shape[0] // 2
    mine, other = half_refs[0][...], half_refs[1][...]
    top_left = jnp.where(core == 0, mine, other)
    low_right = jnp.where(core == 0, other, mine)
    s_ref[:mid, :mid] = own_ref[:mid, :mid] + top_left[:mid, :]
    s_ref[mid:, mid:] = own_ref[mid:, mid:] + low_right[:mid, :]
    s_ref[: mid // 2, mid:] = own_ref[: mid // 2, mid:] + top_left[mid:, :]
    s_ref[mid // 2 : mid, mid:] = own_ref[mid // 2 : mid, mid:] + low_right[mid:, :]
    s_ref[mid:, :mid] = jnp.zeros((mid, mid), F32)
    carried = contract3(halves(coords_ref[...]), halves(top_ref[...]), 0, 1 if first else 0)
    if carried.shape[1] < e_ref.shape[1]:
        e_ref[...] = jnp.zeros(e_ref.shape, F32)
    e_ref[:, : carried.shape[1]] = carried


def node_kernel(first, rank_ref, core_ref, own_ref, mine_ref, other_ref, coords_ref, top_ref, next_own_ref, next_coords_ref, next_top_ref, next_half_ref, s_ref, e_ref):
    core = core_ref[0]
    node_start(first, core, own_ref, (mine_ref, other_ref), coords_ref, top_ref, s_ref, e_ref)
    masked_factor(s_ref, e_ref, rank_ref[0], next_coords_ref, next_top_ref, next_own_ref)
    pack_half(next_own_ref, next_half_ref, core)


def last_node_kernel(first, rank_ref, core_ref, own_ref, mine_ref, other_ref, coords_ref, top_ref, out_ref, s_ref, e_ref, r_ref, x_ref):
    node_start(first, core_ref[0], own_ref, (mine_ref, other_ref), coords_ref, top_ref, s_ref, e_ref)
    masked_factor(s_ref, e_ref, rank_ref[0], r_ref, x_ref)
    out_ref[...] = x_ref[...].T[: out_ref.shape[0], :]


def node(rank, core, own, mine, other, coords, top, share, height):
    width = own.shape[0]
    padded = -(-share // LANES) * LANES
    square = jax.ShapeDtypeStruct((width, width), F32)
    scratch = [pltpu.VMEM((width, width), F32), pltpu.VMEM((width, padded), F32)]
    last = height == LEVELS
    if last:
        kernel, out_shape = last_node_kernel, (jax.ShapeDtypeStruct((share, width), F32),)
        scratch += scratch[:2]
    else:
        kernel = node_kernel
        out_shape = (square, square, jax.ShapeDtypeStruct((width, padded), F32), half_shape(width))
    return pl.pallas_call(
        functools.partial(kernel, height == 1),
        in_specs=[SMEM] * 2 + [VMEM] * 5,
        out_specs=(VMEM,) * len(out_shape),
        out_shape=out_shape,
        scratch_shapes=scratch,
        name="last_node" if last else "node",
    )(rank, core, own, mine, other, coords, top)


def swapped(block, axis, distance):
    count = lax.axis_size(axis)
    route = [(low, low ^ distance) for low in range(count) if low ^ distance < count]
    return lax.ppermute(block, axis, route)


def body(frontal, sketch, rank_table):
    parts = lax.axis_size("col")
    chips = parts // 2
    share = frontal.shape[0] // parts
    row_group = lax.axis_index("row")
    index = lax.axis_index("col").astype(jnp.int32).reshape(1)
    ranks = lax.dynamic_slice_in_dim(rank_table, row_group, 1, 1)

    leaving = partial_samples(index, frontal, sketch, parts, 1)
    arriving = swapped(leaving, "col", 1)
    staying = partial_samples(index, frontal, sketch, parts, 0)
    chip_sum = staying + arriving
    part_of = lambda at: chip_sum[at * share : (at + 1) * share]
    total = part_of(0)
    for other in [swapped(part_of(at), "col", 2 * at) for at in range(1, chips)]:
        total = total + other
    gathered = [total] + [swapped(total, "col", 2 * at) for at in range(1, chips)]
    pieces = []
    for piece in gathered:
        pieces += [piece, swapped(piece, "col", 1)]

    core = index % 2
    inverse, coords, own, half = leaf_factor(ranks[0], core, pieces)
    mine = swapped(half, "row", 1)
    leaf_share, coupling, high, low = first_couplings(index, inverse, frontal, pieces, 4, 2)
    top = leaf_share
    for height in range(1, LEVELS):
        mine, coupling = lax.optimization_barrier((mine, coupling))
        other = swapped(mine, "col", 1)
        own, coords, top, half = node(ranks[height], core, own, mine, other, coords, top, share, height)
        mine = swapped(half, "row", 1 << height)
        if height == 1:
            coupling = more_couplings(high, low, frontal, coupling, half, 4, 2)
    mine, coupling = lax.optimization_barrier((mine, coupling))
    other = swapped(mine, "col", 1)
    (top,) = node(ranks[LEVELS], core, own, mine, other, coords, top, share, LEVELS)
    return (leaf_share, top, coupling)


def solution(mesh):
    return jax.shard_map(
        body,
        mesh=mesh,
        in_specs=(P("row", "col"), P("col", None), P()),
        out_specs=(P(("row", "col"), None), P(("row", "col"), None), P("row", "col")),
        check_vma=False,
    )
```

```python
import functools

import jax
import jax.numpy as jnp
from jax import lax
from jax.experimental import pallas as pl
from jax.experimental.pallas import tpu as pltpu
from jax.sharding import PartitionSpec as P

LEVELS = 2
TILE = 8
GROUP = 16
LANES = 128
F32 = jnp.float32
BF16 = jnp.bfloat16
EXACT = lax.Precision.HIGHEST
VMEM = pl.BlockSpec(memory_space=pltpu.VMEM)
SMEM = pl.BlockSpec(memory_space=pltpu.SMEM)
ROOM = pltpu.CompilerParams(vmem_limit_bytes=28 << 20)


def far(array):
    return pltpu.with_memory_space_constraint(array, pltpu.HBM)


def kept(array):
    return pltpu.with_memory_space_constraint(array, pltpu.VMEM)


def contract(left, right, dim_left, dim_right, precision=None):
    return lax.dot_general(
        left, right, (((dim_left,), (dim_right,)), ((), ())), precision=precision, preferred_element_type=F32
    )


def halves(value):
    high = value.astype(BF16)
    return high, (value - high.astype(F32)).astype(BF16)


def contract3(left, right, dim_left, dim_right):
    (lh, ll), (rh, rl) = left, right
    return (
        contract(lh, rh, dim_left, dim_right)
        + contract(lh, rl, dim_left, dim_right)
        + contract(ll, rh, dim_left, dim_right)
    )


def over_lanes(tile, lane):
    return jnp.broadcast_to(tile[:, lane : lane + 1], tile.shape)


def over_rows(tile, row):
    return jnp.broadcast_to(tile[row : row + 1, :], tile.shape)


def along_lanes(tile, index):
    return jnp.take_along_axis(tile, index, axis=1, mode="promise_in_bounds")


def packed_contract3(left, right):
    (lh, ll), (rh, rl) = left, right
    return contract(jnp.concatenate([lh, lh, ll], axis=0), jnp.concatenate([rh, rl, rh], axis=0), 0, 0)


def eliminate(parts, outs, low, rank, update):
    n = parts[0][0].shape[0]
    at = low - parts[0][1]
    own = GROUP // TILE
    count = min(2 * own, (n - low) // TILE)
    sub = lax.broadcasted_iota(jnp.int32, (TILE, LANES), 0)
    lane = lax.broadcasted_iota(jnp.int32, (TILE, LANES), 1)
    span = lambda t: slice(low + TILE * t, low + TILE * (t + 1))
    work = [[ref[span(t), c : c + LANES] for ref, c in parts] for t in range(count)]
    less = update()
    diag = [over_lanes(work[0][0], at + k) for k in range(TILE)]
    for t in range(own):
        left = rank - (low + TILE * t)
        for k in range(TILE):
            diag[k] = jnp.where((sub < left) & (left > k), diag[k], (sub == k).astype(F32))
        pivots = None
        for j in range(TILE):
            below = [over_rows(diag[k], j) if k >= j else None for k in range(TILE)]
            pivot = below[j]
            scale = 1.0 / pivot
            lower = jnp.where(sub > j, diag[j], 0.0)
            for k in range(j + 1, TILE):
                diag[k] = diag[k] - (lower * below[k]) * scale
            pivots = pivot if pivots is None else jnp.where(sub == j, pivot, pivots)
            scale = jnp.where(left > j, scale, 0.0)
            row = [over_rows(part, j) for part in work[t]]
            scaled = [part * scale for part in row]
            for u in range(t + 1, count):
                ahead_of = at + TILE * u
                column = along_lanes(row[ahead_of // LANES], sub + ahead_of % LANES)
                work[u] = [part - column * other for part, other in zip(work[u], scaled)]
            work[t] = [part - lower * other for part, other in zip(work[t], scaled)]
        root = jnp.where(sub < left, lax.rsqrt(pivots), 0.0)
        for part, (ref, c, upper) in zip(work[t], outs):
            part = part * root
            if upper:
                part = jnp.where(lane + c >= sub + (low + TILE * t), part, 0.0)
            ref[span(t), c : c + LANES] = part
        if t + 1 < own:
            diag = [over_lanes(work[t + 1][0], at + TILE * (t + 1) + k) for k in range(TILE)]
    past = low + GROUP
    for t in range(own, count):
        for q, (ref, c) in enumerate(parts):
            part = work[t][q]
            if less is not None and less[q] is not None:
                part = part - less[q][TILE * (t - own) : TILE * (t - own + 1)]
            ref[span(t), c : c + LANES] = part
    if less is not None:
        for q, (ref, c) in enumerate(parts):
            if less[q] is not None and low + TILE * count < n:
                ref[low + TILE * count :, c : c + LANES] = (
                    ref[low + TILE * count :, c : c + LANES] - less[q][TILE * (count - own) :]
                )


def masked_factor(s_ref, e_ref, rank, coords_ref, x_ref, own_ref=None, growing=False):
    n = s_ref.shape[0]
    wide = e_ref.shape[1]
    coords_ref[...] = jnp.zeros(coords_ref.shape, F32)
    x_ref[...] = jnp.zeros(x_ref.shape, F32)
    if own_ref is not None:
        own_ref[...] = s_ref[...]
    extent_at = lambda low: min(wide, low // LANES * LANES + LANES) if growing else wide
    for low in range(0, n, GROUP):
        slab = low // LANES * LANES
        s_at = list(range(slab, n, LANES))
        e_at = list(range(0, extent_at(low), LANES))
        parts = [(s_ref, c) for c in s_at] + [(e_ref, c) for c in e_at]
        outs = [(coords_ref, c, True) for c in s_at] + [(x_ref, c, False) for c in e_at]

        def update(low=low, slab=slab, s_at=s_at, e_at=e_at):
            past = low + GROUP
            if low == 0 or past >= n:
                return None
            before = slice(low - GROUP, low)
            panel = halves(coords_ref[before, slab:])
            known = extent_at(low - GROUP)
            right = panel
            if known:
                right = tuple(
                    jnp.concatenate(pair, axis=1) for pair in zip(panel, halves(x_ref[before, :known]))
                )
            product = packed_contract3(tuple(part[:, past - slab :] for part in panel), right)
            less = [product[:, c - slab : c - slab + LANES] for c in s_at]
            return less + [
                product[:, n - slab + c : n - slab + c + LANES] if c < known else None for c in e_at
            ]

        pl.when(rank > low)(functools.partial(eliminate, parts, outs, low, rank, update))
    if own_ref is not None:

        @pl.when(rank < n)
        def _():
            rows = lax.broadcasted_iota(jnp.int32, (n, n), 0)
            cols = lax.broadcasted_iota(jnp.int32, (n, n), 1)
            panel = halves(coords_ref[...])
            outside = (rows < rank) | (cols < rank)
            own_ref[...] = jnp.where(outside, own_ref[...], contract3(panel, panel, 0, 0))


def first_samples_kernel(count, index_ref, *refs):
    frontal_refs, (sketch_ref, out_ref, high_ref, low_ref) = refs[:count], refs[count:]

    @pl.when(pl.program_id(0) == 0)
    def _():
        high_ref[...], low_ref[...] = halves(sketch_ref[...])

    samples_kernel(count, index_ref, *frontal_refs, high_ref, low_ref, out_ref)


def samples_kernel(count, index_ref, *refs):
    frontal_refs, (high_ref, low_ref, out_ref) = refs[:count], refs[count:]
    rows = halves(jnp.concatenate([ref[...] for ref in frontal_refs], axis=0))
    size = rows[0].shape[0]
    start = pl.multiple_of(pl.program_id(0) * size, size)
    out_ref[pl.ds(start, size), :] = contract3(rows, (high_ref[...], low_ref[...]), 1, 0)


def partial_samples(index, frontal, sketch, parts, offset, blocks=2):
    share, inner = frontal.shape[0] // parts, frontal.shape[1]
    width = sketch[0].shape[1]
    count = parts // 2 // blocks
    out_shape = (pltpu.VMEM((parts // 2 * share, width), F32),)
    first = len(sketch) == 1
    if first:
        out_shape += (pltpu.VMEM((inner, width), BF16),) * 2

    def rows_of(d):
        return pl.BlockSpec((share, inner), lambda k, index: (index[0] ^ (2 * (count * k + d) + offset), 0))

    return pl.pallas_call(
        functools.partial(first_samples_kernel if first else samples_kernel, count),
        grid_spec=pltpu.PrefetchScalarGridSpec(
            num_scalar_prefetch=1,
            grid=(blocks,),
            in_specs=[rows_of(d) for d in range(count)]
            + ([pl.BlockSpec((inner, width), lambda k, index: (0, 0))] if first else [VMEM, VMEM]),
            out_specs=(VMEM,) * len(out_shape),
        ),
        out_shape=out_shape,
        compiler_params=ROOM,
        name="first_samples" if first else "more_samples",
    )(index, *[far(frontal)] * count, *(sketch if not first else map(far, sketch)))


def unit_matrix(shape):
    rows = lax.broadcasted_iota(jnp.int32, shape, 0)
    cols = lax.broadcasted_iota(jnp.int32, shape, 1)
    return (rows == cols).astype(F32)


def pack_half(square_ref, half_ref, core):
    mid = square_ref.shape[0] // 2
    first = core == 0
    half_ref[:mid, :] = jnp.where(first, square_ref[:mid, :mid], square_ref[mid:, mid:])
    half_ref[mid:, :] = jnp.where(first, square_ref[: mid // 2, mid:], square_ref[mid // 2 : mid, mid:])


def leaf_kernel(rank_ref, core_ref, *refs):
    pieces, (p_ref, coords_ref, own_ref, half_ref, s_ref, e_ref) = refs[:-6], refs[-6:]
    e_ref[...] = unit_matrix(e_ref.shape)
    samples = halves(jnp.concatenate([piece[...] for piece in pieces], axis=0))
    s_ref[...] = contract3(samples, samples, 0, 0)
    masked_factor(s_ref, e_ref, rank_ref[0], coords_ref, p_ref, own_ref, growing=True)
    pack_half(own_ref, half_ref, core_ref[0])


def half_shape(width):
    return pltpu.VMEM((width * 3 // 4, width // 2), F32)


def leaf_factor(rank, core, pieces):
    width = pieces[0].shape[1]
    square = pltpu.VMEM((width, width), F32)
    return pl.pallas_call(
        leaf_kernel,
        in_specs=[SMEM] * 2 + [VMEM] * len(pieces),
        out_specs=(VMEM,) * 4,
        out_shape=(square,) * 3 + (half_shape(width),),
        scratch_shapes=[pltpu.VMEM((width, width), F32)] * 2,
        compiler_params=ROOM,
        name="leaf_factor",
    )(rank, core, *[kept(piece) for piece in pieces])


def first_coupling_kernel(count, index_ref, p_ref, frontal_ref, *refs):
    pieces, (share_ref, out_ref, high_ref, low_ref) = refs[:count], refs[count:]
    share = pieces[0].shape[0]

    @pl.when(pl.program_id(0) == 0)
    def _():
        inverse = halves(p_ref[...])
        for at, piece in enumerate(pieces):
            part = halves(piece[...])
            if at == 0:
                share_ref[...] = contract3(part, inverse, 1, 1)
            start = pl.multiple_of((index_ref[0] ^ at) * share, share)
            high, low = halves(contract3(part, inverse, 1, 1))
            high_ref[pl.ds(start, share), :] = high
            low_ref[pl.ds(start, share), :] = low

    out_ref[...] = contract3((high_ref[...], low_ref[...]), halves(frontal_ref[...]), 0, 0)


def first_couplings(index, inverse, frontal, pieces, blocks, done):
    rows, cols = frontal.shape
    share, width = pieces[0].shape
    split = pltpu.VMEM((rows, width), BF16)
    return pl.pallas_call(
        functools.partial(first_coupling_kernel, len(pieces)),
        grid_spec=pltpu.PrefetchScalarGridSpec(
            num_scalar_prefetch=1,
            grid=(done,),
            in_specs=[VMEM, pl.BlockSpec((rows, cols // blocks), lambda b, index: (0, b))]
            + [VMEM] * len(pieces),
            out_specs=(
                VMEM,
                pl.BlockSpec((width, cols // blocks), lambda b, index: (0, b)),
                VMEM,
                VMEM,
            ),
        ),
        out_shape=(pltpu.VMEM((share, width), F32), jax.ShapeDtypeStruct((width, cols), F32), split, split),
        compiler_params=ROOM,
        name="first_couplings",
    )(index, kept(inverse), far(frontal), *[kept(piece) for piece in pieces])


def more_coupling_kernel(high_ref, low_ref, frontal_ref, before_ref, after_ref, out_ref):
    out_ref[...] = contract3((high_ref[...], low_ref[...]), halves(frontal_ref[...]), 0, 0)


def more_couplings(high, low, frontal, before, after, blocks, done):
    rows, cols = frontal.shape
    width = high.shape[1]
    return pl.pallas_call(
        more_coupling_kernel,
        grid=(blocks - done,),
        in_specs=[
            VMEM,
            VMEM,
            pl.BlockSpec((rows, cols // blocks), lambda b: (0, b + done)),
            pl.BlockSpec(memory_space=pl.ANY),
            pl.BlockSpec(memory_space=pl.ANY),
        ],
        out_specs=pl.BlockSpec((width, cols // blocks), lambda b: (0, b + done)),
        out_shape=jax.ShapeDtypeStruct((width, cols), F32),
        input_output_aliases={3: 0},
        compiler_params=ROOM,
        name="more_couplings",
    )(kept(high), kept(low), frontal, before, after)


def node_start(first, core, own_ref, half_refs, coords_ref, top_ref, s_ref, e_ref):
    mid = own_ref.shape[0] // 2
    mine, other = half_refs[0][...], half_refs[1][...]
    top_left = jnp.where(core == 0, mine, other)
    low_right = jnp.where(core == 0, other, mine)
    s_ref[:mid, :mid] = own_ref[:mid, :mid] + top_left[:mid, :]
    s_ref[mid:, mid:] = own_ref[mid:, mid:] + low_right[:mid, :]
    s_ref[: mid // 2, mid:] = own_ref[: mid // 2, mid:] + top_left[mid:, :]
    s_ref[mid // 2 : mid, mid:] = own_ref[mid // 2 : mid, mid:] + low_right[mid:, :]
    s_ref[mid:, :mid] = jnp.zeros((mid, mid), F32)
    carried = contract3(halves(coords_ref[...]), halves(top_ref[...]), 0, 1 if first else 0)
    if carried.shape[1] < e_ref.shape[1]:
        e_ref[...] = jnp.zeros(e_ref.shape, F32)
    e_ref[:, : carried.shape[1]] = carried


def node_kernel(first, rank_ref, core_ref, own_ref, mine_ref, other_ref, coords_ref, top_ref, next_own_ref, next_coords_ref, next_top_ref, next_half_ref, s_ref, e_ref):
    core = core_ref[0]
    node_start(first, core, own_ref, (mine_ref, other_ref), coords_ref, top_ref, s_ref, e_ref)
    masked_factor(s_ref, e_ref, rank_ref[0], next_coords_ref, next_top_ref, next_own_ref)
    pack_half(next_own_ref, next_half_ref, core)


def last_node_kernel(first, rank_ref, core_ref, own_ref, mine_ref, other_ref, coords_ref, top_ref, out_ref, s_ref, e_ref, r_ref, x_ref):
    node_start(first, core_ref[0], own_ref, (mine_ref, other_ref), coords_ref, top_ref, s_ref, e_ref)
    masked_factor(s_ref, e_ref, rank_ref[0], r_ref, x_ref)
    out_ref[...] = x_ref[...].T[: out_ref.shape[0], :]


def node(rank, core, own, mine, other, coords, top, share, height):
    width = own.shape[0]
    padded = -(-share // LANES) * LANES
    square = pltpu.VMEM((width, width), F32)
    scratch = [pltpu.VMEM((width, width), F32), pltpu.VMEM((width, padded), F32)]
    last = height == LEVELS
    if last:
        kernel, out_shape = last_node_kernel, (jax.ShapeDtypeStruct((share, width), F32),)
        scratch += scratch[:2]
    else:
        kernel = node_kernel
        out_shape = (square, square, pltpu.VMEM((width, padded), F32), half_shape(width))
    return pl.pallas_call(
        functools.partial(kernel, height == 1),
        in_specs=[SMEM] * 2 + [VMEM] * 5,
        out_specs=(VMEM,) * len(out_shape),
        out_shape=out_shape,
        scratch_shapes=scratch,
        compiler_params=ROOM,
        name="last_node" if last else "node",
    )(rank, core, *[kept(array) for array in (own, mine, other, coords, top)])


def swapped(block, axis, distance):
    count = lax.axis_size(axis)
    route = [(low, low ^ distance) for low in range(count) if low ^ distance < count]
    return lax.ppermute(block, axis, route)


def body(frontal, sketch, rank_table):
    parts = lax.axis_size("col")
    chips = parts // 2
    share = frontal.shape[0] // parts
    row_group = lax.axis_index("row")
    index = lax.axis_index("col").astype(jnp.int32).reshape(1)
    ranks = lax.dynamic_slice_in_dim(rank_table, row_group, 1, 1)

    leaving, *split = partial_samples(index, frontal, (sketch,), parts, 1)
    arriving = swapped(leaving, "col", 1)
    (staying,) = partial_samples(index, frontal, tuple(kept(part) for part in split), parts, 0)
    chip_sum = staying + arriving
    part_of = lambda at: chip_sum[at * share : (at + 1) * share]
    total = part_of(0)
    for other in [swapped(part_of(at), "col", 2 * at) for at in range(1, chips)]:
        total = total + other
    gathered = [total] + [swapped(total, "col", 2 * at) for at in range(1, chips)]
    pieces = []
    for piece in gathered:
        pieces += [piece, swapped(piece, "col", 1)]

    core = index % 2
    inverse, coords, own, half = leaf_factor(ranks[0], core, pieces)
    mine = swapped(half, "row", 1)
    leaf_share, coupling, high, low = first_couplings(index, inverse, frontal, pieces, 4, 1)
    top = leaf_share
    for height in range(1, LEVELS):
        mine, coupling = lax.optimization_barrier((mine, coupling))
        other = swapped(mine, "col", 1)
        own, coords, top, half = node(ranks[height], core, own, mine, other, coords, top, share, height)
        mine = swapped(half, "row", 1 << height)
        if height == 1:
            coupling = more_couplings(high, low, frontal, coupling, half, 4, 1)
    mine, coupling = lax.optimization_barrier((mine, coupling))
    other = swapped(mine, "col", 1)
    (top,) = node(ranks[LEVELS], core, own, mine, other, coords, top, share, LEVELS)
    return (leaf_share, top, coupling)


def solution(mesh):
    return jax.shard_map(
        body,
        mesh=mesh,
        in_specs=(P("row", "col"), P("col", None), P()),
        out_specs=(P(("row", "col"), None), P(("row", "col"), None), P("row", "col")),
        check_vma=False,
    )
```

```python
import functools

import jax
import jax.numpy as jnp
from jax import lax
from jax.experimental import pallas as pl
from jax.experimental.pallas import tpu as pltpu
from jax.sharding import PartitionSpec as P

LEVELS = 2
TILE = 8
GROUP = 16
LANES = 128
F32 = jnp.float32
BF16 = jnp.bfloat16
EXACT = lax.Precision.HIGHEST
VMEM = pl.BlockSpec(memory_space=pltpu.VMEM)
SMEM = pl.BlockSpec(memory_space=pltpu.SMEM)
ROOM = pltpu.CompilerParams(vmem_limit_bytes=28 << 20)


def far(array):
    return pltpu.with_memory_space_constraint(array, pltpu.HBM)


def kept(array):
    return pltpu.with_memory_space_constraint(array, pltpu.VMEM)


def contract(left, right, dim_left, dim_right, precision=None):
    return lax.dot_general(
        left, right, (((dim_left,), (dim_right,)), ((), ())), precision=precision, preferred_element_type=F32
    )


def halves(value):
    high = value.astype(BF16)
    return high, (value - high.astype(F32)).astype(BF16)


def contract3(left, right, dim_left, dim_right):
    (lh, ll), (rh, rl) = left, right
    return (
        contract(lh, rh, dim_left, dim_right)
        + contract(lh, rl, dim_left, dim_right)
        + contract(ll, rh, dim_left, dim_right)
    )


def over_lanes(tile, lane):
    return jnp.broadcast_to(tile[:, lane : lane + 1], tile.shape)


def over_rows(tile, row):
    return jnp.broadcast_to(tile[row : row + 1, :], tile.shape)


def along_lanes(tile, index):
    return jnp.take_along_axis(tile, index, axis=1, mode="promise_in_bounds")


def packed_contract3(left, right):
    (lh, ll), (rh, rl) = left, right
    return contract(jnp.concatenate([lh, lh, ll], axis=0), jnp.concatenate([rh, rl, rh], axis=0), 0, 0)


def eliminate(parts, outs, low, rank, update):
    n = parts[0][0].shape[0]
    at = low - parts[0][1]
    own = GROUP // TILE
    count = min(2 * own, (n - low) // TILE)
    sub = lax.broadcasted_iota(jnp.int32, (TILE, LANES), 0)
    lane = lax.broadcasted_iota(jnp.int32, (TILE, LANES), 1)
    span = lambda t: slice(low + TILE * t, low + TILE * (t + 1))
    work = [[ref[span(t), c : c + LANES] for ref, c in parts] for t in range(count)]
    less = update()
    diag = [over_lanes(work[0][0], at + k) for k in range(TILE)]
    for t in range(own):
        left = rank - (low + TILE * t)
        for k in range(TILE):
            diag[k] = jnp.where((sub < left) & (left > k), diag[k], (sub == k).astype(F32))
        pivots = None
        for j in range(TILE):
            below = [over_rows(diag[k], j) if k >= j else None for k in range(TILE)]
            pivot = below[j]
            scale = 1.0 / pivot
            lower = jnp.where(sub > j, diag[j], 0.0)
            for k in range(j + 1, TILE):
                diag[k] = diag[k] - (lower * below[k]) * scale
            pivots = pivot if pivots is None else jnp.where(sub == j, pivot, pivots)
            scale = jnp.where(left > j, scale, 0.0)
            row = [over_rows(part, j) for part in work[t]]
            scaled = [part * scale for part in row]
            for u in range(t + 1, count):
                ahead_of = at + TILE * u
                column = along_lanes(row[ahead_of // LANES], sub + ahead_of % LANES)
                work[u] = [part - column * other for part, other in zip(work[u], scaled)]
            work[t] = [part - lower * other for part, other in zip(work[t], scaled)]
        root = jnp.where(sub < left, lax.rsqrt(pivots), 0.0)
        for part, (ref, c, upper) in zip(work[t], outs):
            part = part * root
            if upper:
                part = jnp.where(lane + c >= sub + (low + TILE * t), part, 0.0)
            ref[span(t), c : c + LANES] = part
        if t + 1 < own:
            diag = [over_lanes(work[t + 1][0], at + TILE * (t + 1) + k) for k in range(TILE)]
    past = low + GROUP
    for t in range(own, count):
        for q, (ref, c) in enumerate(parts):
            part = work[t][q]
            if less is not None and less[q] is not None and TILE * (t - own) < less[q].shape[0]:
                part = part - less[q][TILE * (t - own) : TILE * (t - own + 1)]
            ref[span(t), c : c + LANES] = part
    if less is not None:
        for q, (ref, c) in enumerate(parts):
            if less[q] is not None:
                begin, end = low + TILE * count, past + less[q].shape[0]
                if begin < end:
                    ref[begin:end, c : c + LANES] = ref[begin:end, c : c + LANES] - less[q][begin - past :]


def masked_factor(s_ref, e_ref, rank, coords_ref, x_ref, own_ref=None, growing=False):
    n = s_ref.shape[0]
    wide = e_ref.shape[1]
    coords_ref[...] = jnp.zeros(coords_ref.shape, F32)
    x_ref[...] = jnp.zeros(x_ref.shape, F32)
    if own_ref is not None:
        own_ref[...] = s_ref[...]
    extent_at = lambda low: min(wide, low // LANES * LANES + LANES) if growing else wide
    for low in range(0, n, GROUP):
        slab = low // LANES * LANES
        s_at = list(range(slab, n, LANES))
        e_at = list(range(0, extent_at(low), LANES))
        parts = [(s_ref, c) for c in s_at] + [(e_ref, c) for c in e_at]
        outs = [(coords_ref, c, True) for c in s_at] + [(x_ref, c, False) for c in e_at]

        def update(low=low, slab=slab, s_at=s_at, e_at=e_at):
            past = low + GROUP
            if low == 0 or past >= n:
                return None
            before = slice(low - GROUP, low)
            panel = halves(coords_ref[before, slab:])
            known = extent_at(low - GROUP)
            right = panel
            if known:
                right = tuple(
                    jnp.concatenate(pair, axis=1) for pair in zip(panel, halves(x_ref[before, :known]))
                )
            left = tuple(part[:, past - slab :] for part in panel)
            cut = slab + LANES - past
            if cut <= 0 or slab + LANES == n:
                product = packed_contract3(left, right)
                less = [product[:, c - slab : c - slab + LANES] for c in s_at]
            else:
                upper = packed_contract3(tuple(part[:, :cut] for part in left), tuple(part[:, :LANES] for part in right))
                product = packed_contract3(left, tuple(part[:, LANES:] for part in right))
                product = jnp.concatenate([jnp.zeros((product.shape[0], LANES), F32), product], axis=1)
                less = [upper] + [product[:, c - slab : c - slab + LANES] for c in s_at[1:]]
            return less + [
                product[:, n - slab + c : n - slab + c + LANES] if c < known else None for c in e_at
            ]

        pl.when(rank > low)(functools.partial(eliminate, parts, outs, low, rank, update))
    if own_ref is not None:

        @pl.when(rank < n)
        def _():
            rows = lax.broadcasted_iota(jnp.int32, (n, n), 0)
            cols = lax.broadcasted_iota(jnp.int32, (n, n), 1)
            panel = halves(coords_ref[...])
            outside = (rows < rank) | (cols < rank)
            own_ref[...] = jnp.where(outside, own_ref[...], contract3(panel, panel, 0, 0))


def first_samples_kernel(count, index_ref, *refs):
    frontal_refs, (sketch_ref, out_ref, high_ref, low_ref) = refs[:count], refs[count:]

    @pl.when(pl.program_id(0) == 0)
    def _():
        high_ref[...], low_ref[...] = halves(sketch_ref[...])

    samples_kernel(count, index_ref, *frontal_refs, high_ref, low_ref, out_ref)


def samples_kernel(count, index_ref, *refs):
    frontal_refs, (high_ref, low_ref, out_ref) = refs[:count], refs[count:]
    rows = halves(jnp.concatenate([ref[...] for ref in frontal_refs], axis=0))
    size = rows[0].shape[0]
    start = pl.multiple_of(pl.program_id(0) * size, size)
    out_ref[pl.ds(start, size), :] = contract3(rows, (high_ref[...], low_ref[...]), 1, 0)


def partial_samples(index, frontal, sketch, parts, offset, blocks=2):
    share, inner = frontal.shape[0] // parts, frontal.shape[1]
    width = sketch[0].shape[1]
    count = parts // 2 // blocks
    out_shape = (pltpu.VMEM((parts // 2 * share, width), F32),)
    first = len(sketch) == 1
    if first:
        out_shape += (pltpu.VMEM((inner, width), BF16),) * 2

    def rows_of(d):
        return pl.BlockSpec((share, inner), lambda k, index: (index[0] ^ (2 * (count * k + d) + offset), 0))

    return pl.pallas_call(
        functools.partial(first_samples_kernel if first else samples_kernel, count),
        grid_spec=pltpu.PrefetchScalarGridSpec(
            num_scalar_prefetch=1,
            grid=(blocks,),
            in_specs=[rows_of(d) for d in range(count)]
            + ([pl.BlockSpec((inner, width), lambda k, index: (0, 0))] if first else [VMEM, VMEM]),
            out_specs=(VMEM,) * len(out_shape),
        ),
        out_shape=out_shape,
        compiler_params=ROOM,
        name="first_samples" if first else "more_samples",
    )(index, *[far(frontal)] * count, *(sketch if not first else map(far, sketch)))


def unit_matrix(shape):
    rows = lax.broadcasted_iota(jnp.int32, shape, 0)
    cols = lax.broadcasted_iota(jnp.int32, shape, 1)
    return (rows == cols).astype(F32)


def pack_half(square_ref, half_ref, core):
    mid = square_ref.shape[0] // 2
    first = core == 0
    half_ref[:mid, :] = jnp.where(first, square_ref[:mid, :mid], square_ref[mid:, mid:])
    half_ref[mid:, :] = jnp.where(first, square_ref[: mid // 2, mid:], square_ref[mid // 2 : mid, mid:])


def leaf_kernel(rank_ref, at_ref, *refs):
    pieces, (p_ref, coords_ref, own_ref, half_ref, s_ref, e_ref) = refs[:-6], refs[-6:]
    e_ref[...] = unit_matrix(e_ref.shape)
    samples = halves(jnp.concatenate([piece[...] for piece in pieces], axis=0))
    s_ref[...] = contract3(samples, samples, 0, 0)
    masked_factor(s_ref, e_ref, rank_ref[0, at_ref[0]], coords_ref, p_ref, own_ref, growing=True)
    pack_half(own_ref, half_ref, at_ref[1])


def half_shape(width):
    return pltpu.VMEM((width * 3 // 4, width // 2), F32)


def leaf_factor(ranks, place, pieces):
    width = pieces[0].shape[1]
    square = pltpu.VMEM((width, width), F32)
    return pl.pallas_call(
        leaf_kernel,
        in_specs=[SMEM] * 2 + [VMEM] * len(pieces),
        out_specs=(VMEM,) * 4,
        out_shape=(square,) * 3 + (half_shape(width),),
        scratch_shapes=[pltpu.VMEM((width, width), F32)] * 2,
        compiler_params=ROOM,
        name="leaf_factor",
    )(ranks, place, *[kept(piece) for piece in pieces])


def first_coupling_kernel(count, index_ref, p_ref, frontal_ref, *refs):
    pieces, (share_ref, near_ref, out_ref, high_ref, low_ref) = refs[:count], refs[count:]
    share = pieces[0].shape[0]

    @pl.when(pl.program_id(0) == 0)
    def _():
        inverse = halves(p_ref[...])
        for at, piece in enumerate(pieces):
            part = halves(piece[...])
            if at == 0:
                near_ref[...] = contract3(part, inverse, 1, 1)
                share_ref[...] = near_ref[...]
            start = pl.multiple_of((index_ref[0] ^ at) * share, share)
            high, low = halves(contract3(part, inverse, 1, 1))
            high_ref[pl.ds(start, share), :] = high
            low_ref[pl.ds(start, share), :] = low

    out_ref[...] = contract3((high_ref[...], low_ref[...]), halves(frontal_ref[...]), 0, 0)


def first_couplings(index, inverse, frontal, pieces, blocks, done):
    rows, cols = frontal.shape
    share, width = pieces[0].shape
    split = pltpu.VMEM((rows, width), BF16)
    return pl.pallas_call(
        functools.partial(first_coupling_kernel, len(pieces)),
        grid_spec=pltpu.PrefetchScalarGridSpec(
            num_scalar_prefetch=1,
            grid=(done,),
            in_specs=[VMEM, pl.BlockSpec((rows, cols // blocks), lambda b, index: (0, b))]
            + [VMEM] * len(pieces),
            out_specs=(
                pl.BlockSpec((share, width), lambda b, index: (0, 0)),
                VMEM,
                pl.BlockSpec((width, cols // blocks), lambda b, index: (0, b)),
                VMEM,
                VMEM,
            ),
        ),
        out_shape=(
            jax.ShapeDtypeStruct((share, width), F32),
            pltpu.VMEM((share, width), F32),
            jax.ShapeDtypeStruct((width, cols), F32),
            split,
            split,
        ),
        compiler_params=ROOM,
        name="first_couplings",
    )(index, kept(inverse), far(frontal), *[kept(piece) for piece in pieces])


def more_coupling_kernel(high_ref, low_ref, frontal_ref, before_ref, after_ref, out_ref):
    out_ref[...] = contract3((high_ref[...], low_ref[...]), halves(frontal_ref[...]), 0, 0)


def more_couplings(high, low, frontal, before, after, blocks, done):
    rows, cols = frontal.shape
    width = high.shape[1]
    return pl.pallas_call(
        more_coupling_kernel,
        grid=(blocks - done,),
        in_specs=[
            VMEM,
            VMEM,
            pl.BlockSpec((rows, cols // blocks), lambda b: (0, b + done)),
            pl.BlockSpec(memory_space=pl.ANY),
            pl.BlockSpec(memory_space=pl.ANY),
        ],
        out_specs=pl.BlockSpec((width, cols // blocks), lambda b: (0, b + done)),
        out_shape=jax.ShapeDtypeStruct((width, cols), F32),
        input_output_aliases={3: 0},
        compiler_params=ROOM,
        name="more_couplings",
    )(kept(high), kept(low), frontal, before, after)


def node_start(first, core, own_ref, half_refs, coords_ref, top_ref, s_ref, e_ref):
    mid = own_ref.shape[0] // 2
    mine, other = half_refs[0][...], half_refs[1][...]
    top_left = jnp.where(core == 0, mine, other)
    low_right = jnp.where(core == 0, other, mine)
    s_ref[:mid, :mid] = own_ref[:mid, :mid] + top_left[:mid, :]
    s_ref[mid:, mid:] = own_ref[mid:, mid:] + low_right[:mid, :]
    s_ref[: mid // 2, mid:] = own_ref[: mid // 2, mid:] + top_left[mid:, :]
    s_ref[mid // 2 : mid, mid:] = own_ref[mid // 2 : mid, mid:] + low_right[mid:, :]
    s_ref[mid:, :mid] = jnp.zeros((mid, mid), F32)
    carried = contract3(halves(coords_ref[...]), halves(top_ref[...]), 0, 1 if first else 0)
    if carried.shape[1] < e_ref.shape[1]:
        e_ref[...] = jnp.zeros(e_ref.shape, F32)
    e_ref[:, : carried.shape[1]] = carried


def node_kernel(height, rank_ref, at_ref, own_ref, mine_ref, other_ref, coords_ref, top_ref, next_own_ref, next_coords_ref, next_top_ref, next_half_ref, s_ref, e_ref):
    core = at_ref[1]
    node_start(height == 1, core, own_ref, (mine_ref, other_ref), coords_ref, top_ref, s_ref, e_ref)
    masked_factor(s_ref, e_ref, rank_ref[height, at_ref[0]], next_coords_ref, next_top_ref, next_own_ref)
    pack_half(next_own_ref, next_half_ref, core)


def last_node_kernel(height, rank_ref, at_ref, own_ref, mine_ref, other_ref, coords_ref, top_ref, out_ref, s_ref, e_ref, r_ref, x_ref):
    node_start(height == 1, at_ref[1], own_ref, (mine_ref, other_ref), coords_ref, top_ref, s_ref, e_ref)
    masked_factor(s_ref, e_ref, rank_ref[height, at_ref[0]], r_ref, x_ref)
    out_ref[...] = x_ref[...].T[: out_ref.shape[0], :]


def node(ranks, place, own, mine, other, coords, top, share, height):
    width = own.shape[0]
    padded = -(-share // LANES) * LANES
    square = pltpu.VMEM((width, width), F32)
    scratch = [pltpu.VMEM((width, width), F32), pltpu.VMEM((width, padded), F32)]
    last = height == LEVELS
    if last:
        kernel, out_shape = last_node_kernel, (jax.ShapeDtypeStruct((share, width), F32),)
        scratch += scratch[:2]
    else:
        kernel = node_kernel
        out_shape = (square, square, pltpu.VMEM((width, padded), F32), half_shape(width))
    return pl.pallas_call(
        functools.partial(kernel, height),
        in_specs=[SMEM] * 2 + [VMEM] * 5,
        out_specs=(VMEM,) * len(out_shape),
        out_shape=out_shape,
        scratch_shapes=scratch,
        compiler_params=ROOM,
        name="last_node" if last else "node",
    )(ranks, place, *[kept(array) for array in (own, mine, other, coords, top)])


def swapped(block, axis, distance):
    count = lax.axis_size(axis)
    route = [(low, low ^ distance) for low in range(count) if low ^ distance < count]
    return lax.ppermute(block, axis, route)


def body(frontal, sketch, rank_table):
    parts = lax.axis_size("col")
    chips = parts // 2
    share = frontal.shape[0] // parts
    index = lax.axis_index("col").astype(jnp.int32).reshape(1)
    place = jnp.stack([lax.axis_index("row").astype(jnp.int32), index[0] % 2])

    leaving, *split = partial_samples(index, frontal, (sketch,), parts, 1)
    arriving = swapped(leaving, "col", 1)
    (staying,) = partial_samples(index, frontal, tuple(kept(part) for part in split), parts, 0)
    chip_sum = staying + arriving
    part_of = lambda at: chip_sum[at * share : (at + 1) * share]
    total = part_of(0)
    for other in [swapped(part_of(at), "col", 2 * at) for at in range(1, chips)]:
        total = total + other
    gathered = [total] + [swapped(total, "col", 2 * at) for at in range(1, chips)]
    pieces = []
    for piece in gathered:
        pieces += [piece, swapped(piece, "col", 1)]

    inverse, coords, own, half = leaf_factor(rank_table, place, pieces)
    mine = swapped(half, "row", 1)
    leaf_share, top, coupling, high, low = first_couplings(index, inverse, frontal, pieces, 4, 1)
    for height in range(1, LEVELS):
        mine, coupling = lax.optimization_barrier((mine, coupling))
        other = swapped(mine, "col", 1)
        own, coords, top, half = node(rank_table, place, own, mine, other, coords, top, share, height)
        mine = swapped(half, "row", 1 << height)
        if height == 1:
            coupling = more_couplings(high, low, frontal, coupling, half, 4, 1)
    mine, coupling = lax.optimization_barrier((mine, coupling))
    other = swapped(mine, "col", 1)
    (top,) = node(rank_table, place, own, mine, other, coords, top, share, LEVELS)
    return (leaf_share, top, coupling)


def solution(mesh):
    return jax.shard_map(
        body,
        mesh=mesh,
        in_specs=(P("row", "col"), P("col", None), P()),
        out_specs=(P(("row", "col"), None), P(("row", "col"), None), P("row", "col")),
        check_vma=False,
    )
```

```python
import functools

import jax
import jax.numpy as jnp
from jax import lax
from jax.experimental import pallas as pl
from jax.experimental.pallas import tpu as pltpu
from jax.sharding import PartitionSpec as P


LEVELS = 2
TILE = 8
GROUP = 16
LANES = 128
F32 = jnp.float32
BF16 = jnp.bfloat16
VMEM = pl.BlockSpec(memory_space=pltpu.VMEM)
SMEM = pl.BlockSpec(memory_space=pltpu.SMEM)
ROOM = pltpu.CompilerParams(vmem_limit_bytes=28 << 20)


def far(array):
    return pltpu.with_memory_space_constraint(array, pltpu.HBM)


def kept(array):
    return pltpu.with_memory_space_constraint(array, pltpu.VMEM)


def contract(left, right, dim_left, dim_right, precision=None):
    return lax.dot_general(
        left, right, (((dim_left,), (dim_right,)), ((), ())), precision=precision, preferred_element_type=F32
    )


def halves(value):
    high = value.astype(BF16)
    return high, (value - high.astype(F32)).astype(BF16)


def contract3(left, right, dim_left, dim_right):
    (lh, ll), (rh, rl) = left, right
    return (
        contract(lh, rh, dim_left, dim_right)
        + contract(lh, rl, dim_left, dim_right)
        + contract(ll, rh, dim_left, dim_right)
    )


def over_lanes(tile, lane):
    return jnp.broadcast_to(tile[:, lane : lane + 1], tile.shape)


def over_rows(tile, row):
    return jnp.broadcast_to(tile[row : row + 1, :], tile.shape)


def along_lanes(tile, index):
    return jnp.take_along_axis(tile, index, axis=1, mode="promise_in_bounds")


def packed_contract3(left, right):
    (lh, ll), (rh, rl) = left, right
    return contract(jnp.concatenate([lh, lh, ll], axis=0), jnp.concatenate([rh, rl, rh], axis=0), 0, 0)


def eliminate(parts, outs, low, rank, update):
    n = parts[0][0].shape[0]
    at = low - parts[0][1]
    own = GROUP // TILE
    count = min(2 * own, (n - low) // TILE)
    sub = lax.broadcasted_iota(jnp.int32, (TILE, LANES), 0)
    lane = lax.broadcasted_iota(jnp.int32, (TILE, LANES), 1)
    span = lambda t: slice(low + TILE * t, low + TILE * (t + 1))
    work = [[ref[span(t), c : c + LANES] for ref, c in parts] for t in range(count)]
    less = update()
    diag = [over_lanes(work[0][0], at + k) for k in range(TILE)]
    for t in range(own):
        left = rank - (low + TILE * t)
        cols = ahead = None
        if t + 1 < own:
            cols = [over_lanes(work[t + 1][0], at + TILE * t + k) for k in range(TILE)]
            ahead = [over_lanes(work[t + 1][0], at + TILE * (t + 1) + k) for k in range(TILE)]
        for k in range(TILE):
            diag[k] = jnp.where((sub < left) & (left > k), diag[k], (sub == k).astype(F32))
        pivots = None
        pivot = over_rows(diag[0], 0)
        for j in range(TILE):
            below = [over_rows(diag[k], j) if k > j else None for k in range(TILE)]
            scale = 1.0 / pivot
            lower = jnp.where(sub > j, diag[j], 0.0)
            pivots = pivot if pivots is None else jnp.where(sub == j, pivot, pivots)
            if j + 1 < TILE:
                pivot = over_rows(diag[j + 1], j + 1) - over_rows(diag[j], j + 1) * below[j + 1] * scale
            for k in range(j + 1, TILE):
                diag[k] = diag[k] - (lower * below[k]) * scale
            scale = jnp.where(left > j, scale, 0.0)
            row = [over_rows(part, j) for part in work[t]]
            scaled = [part * scale for part in row]
            for u in range(t + 1, count):
                ahead_of = at + TILE * u
                if u == t + 1 and cols is not None:
                    column = cols[j]
                    column_scaled = column * scale
                    for k in range(j + 1, TILE):
                        cols[k] = cols[k] - column_scaled * below[k]
                    for k in range(TILE):
                        ahead[k] = ahead[k] - column_scaled * over_rows(column, k)
                else:
                    column = along_lanes(row[ahead_of // LANES], sub + ahead_of % LANES)
                work[u] = [part - column * other for part, other in zip(work[u], scaled)]
            work[t] = [part - lower * other for part, other in zip(work[t], scaled)]
        root = jnp.where(sub < left, lax.rsqrt(pivots), 0.0)
        for part, (ref, c, upper) in zip(work[t], outs):
            part = part * root
            if upper:
                part = jnp.where(lane + c >= sub + (low + TILE * t), part, 0.0)
            ref[span(t), c : c + LANES] = part
        if t + 1 < own:
            diag = ahead
    past = low + GROUP
    for t in range(own, count):
        for q, (ref, c) in enumerate(parts):
            part = work[t][q]
            if less is not None and less[q] is not None and TILE * (t - own) < less[q].shape[0]:
                part = part - less[q][TILE * (t - own) : TILE * (t - own + 1)]
            ref[span(t), c : c + LANES] = part
    if less is not None:
        for q, (ref, c) in enumerate(parts):
            if less[q] is not None:
                begin, end = low + TILE * count, past + less[q].shape[0]
                if begin < end:
                    ref[begin:end, c : c + LANES] = ref[begin:end, c : c + LANES] - less[q][begin - past :]


def masked_factor(s_ref, e_ref, rank, coords_ref, x_ref, own_ref=None, growing=False):
    n = s_ref.shape[0]
    wide = e_ref.shape[1]
    coords_ref[...] = jnp.zeros(coords_ref.shape, F32)
    x_ref[...] = jnp.zeros(x_ref.shape, F32)
    if own_ref is not None:
        own_ref[...] = s_ref[...]
    extent_at = lambda low: min(wide, low // LANES * LANES + LANES) if growing else wide
    for low in range(0, n, GROUP):
        slab = low // LANES * LANES
        s_at = list(range(slab, n, LANES))
        e_at = list(range(0, extent_at(low), LANES))
        parts = [(s_ref, c) for c in s_at] + [(e_ref, c) for c in e_at]
        outs = [(coords_ref, c, True) for c in s_at] + [(x_ref, c, False) for c in e_at]

        def update(low=low, slab=slab, s_at=s_at, e_at=e_at):
            past = low + GROUP
            if low == 0 or past >= n:
                return None
            before = slice(low - GROUP, low)
            panel = halves(coords_ref[before, slab:])
            known = extent_at(low - GROUP)
            right = panel
            if known:
                right = tuple(
                    jnp.concatenate(pair, axis=1) for pair in zip(panel, halves(x_ref[before, :known]))
                )
            left = tuple(part[:, past - slab :] for part in panel)
            cut = slab + LANES - past
            if cut <= 0 or slab + LANES == n:
                product = packed_contract3(left, right)
                less = [product[:, c - slab : c - slab + LANES] for c in s_at]
            else:
                upper = packed_contract3(tuple(part[:, :cut] for part in left), tuple(part[:, :LANES] for part in right))
                product = packed_contract3(left, tuple(part[:, LANES:] for part in right))
                product = jnp.concatenate([jnp.zeros((product.shape[0], LANES), F32), product], axis=1)
                less = [upper] + [product[:, c - slab : c - slab + LANES] for c in s_at[1:]]
            return less + [
                product[:, n - slab + c : n - slab + c + LANES] if c < known else None for c in e_at
            ]

        pl.when(rank > low)(functools.partial(eliminate, parts, outs, low, rank, update))
    if own_ref is not None:

        @pl.when(rank < n)
        def _():
            rows = lax.broadcasted_iota(jnp.int32, (n, n), 0)
            cols = lax.broadcasted_iota(jnp.int32, (n, n), 1)
            panel = halves(coords_ref[...])
            outside = (rows < rank) | (cols < rank)
            own_ref[...] = jnp.where(outside, own_ref[...], contract3(panel, panel, 0, 0))


def first_samples_kernel(count, index_ref, *refs):
    frontal_refs, (sketch_ref, out_ref, high_ref, low_ref) = refs[:count], refs[count:]

    @pl.when(pl.program_id(0) == 0)
    def _():
        high_ref[...], low_ref[...] = halves(sketch_ref[...])

    samples_kernel(count, index_ref, *frontal_refs, high_ref, low_ref, out_ref)


def samples_kernel(count, index_ref, *refs):
    frontal_refs, (high_ref, low_ref, out_ref) = refs[:count], refs[count:]
    rows = halves(jnp.concatenate([ref[...] for ref in frontal_refs], axis=0))
    size = rows[0].shape[0]
    start = pl.multiple_of(pl.program_id(0) * size, size)
    out_ref[pl.ds(start, size), :] = contract3(rows, (high_ref[...], low_ref[...]), 1, 0)


def partial_samples(index, frontal, sketch, parts, offset, blocks=2):
    share, inner = frontal.shape[0] // parts, frontal.shape[1]
    width = sketch[0].shape[1]
    count = parts // 2 // blocks
    out_shape = (pltpu.VMEM((parts // 2 * share, width), F32),)
    first = len(sketch) == 1
    if first:
        out_shape += (pltpu.VMEM((inner, width), BF16),) * 2

    def rows_of(d):
        return pl.BlockSpec((share, inner), lambda k, index: (index[0] ^ (2 * (count * k + d) + offset), 0))

    return pl.pallas_call(
        functools.partial(first_samples_kernel if first else samples_kernel, count),
        grid_spec=pltpu.PrefetchScalarGridSpec(
            num_scalar_prefetch=1,
            grid=(blocks,),
            in_specs=[rows_of(d) for d in range(count)]
            + ([pl.BlockSpec((inner, width), lambda k, index: (0, 0))] if first else [VMEM, VMEM]),
            out_specs=(VMEM,) * len(out_shape),
        ),
        out_shape=out_shape,
        compiler_params=ROOM,
        name="first_samples" if first else "more_samples",
    )(index, *[far(frontal)] * count, *(sketch if not first else map(far, sketch)))


def unit_matrix(shape):
    rows = lax.broadcasted_iota(jnp.int32, shape, 0)
    cols = lax.broadcasted_iota(jnp.int32, shape, 1)
    return (rows == cols).astype(F32)


def pack_half(square_ref, half_ref, core):
    mid = square_ref.shape[0] // 2
    first = core == 0
    half_ref[:mid, :] = jnp.where(first, square_ref[:mid, :mid], square_ref[mid:, mid:])
    half_ref[mid:, :] = jnp.where(first, square_ref[: mid // 2, mid:], square_ref[mid // 2 : mid, mid:])


def leaf_kernel(rank_ref, core_ref, *refs):
    pieces, (p_ref, coords_ref, own_ref, half_ref, s_ref, e_ref) = refs[:-6], refs[-6:]
    e_ref[...] = unit_matrix(e_ref.shape)
    samples = halves(jnp.concatenate([piece[...] for piece in pieces], axis=0))
    s_ref[...] = contract3(samples, samples, 0, 0)
    masked_factor(s_ref, e_ref, rank_ref[0], coords_ref, p_ref, own_ref, growing=True)
    pack_half(own_ref, half_ref, core_ref[0])


def half_shape(width):
    return pltpu.VMEM((width * 3 // 4, width // 2), F32)


def leaf_factor(rank, core, pieces):
    width = pieces[0].shape[1]
    square = pltpu.VMEM((width, width), F32)
    return pl.pallas_call(
        leaf_kernel,
        in_specs=[SMEM] * 2 + [VMEM] * len(pieces),
        out_specs=(VMEM,) * 4,
        out_shape=(square,) * 3 + (half_shape(width),),
        scratch_shapes=[pltpu.VMEM((width, width), F32)] * 2,
        compiler_params=ROOM,
        name="leaf_factor",
    )(rank, core, *[kept(piece) for piece in pieces])


def first_coupling_kernel(count, index_ref, p_ref, frontal_ref, *refs):
    pieces, (share_ref, near_ref, out_ref, high_ref, low_ref) = refs[:count], refs[count:]
    share = pieces[0].shape[0]

    @pl.when(pl.program_id(0) == 0)
    def _():
        inverse = halves(p_ref[...])
        for at, piece in enumerate(pieces):
            part = halves(piece[...])
            if at == 0:
                near_ref[...] = contract3(part, inverse, 1, 1)
                share_ref[...] = near_ref[...]
            start = pl.multiple_of((index_ref[0] ^ at) * share, share)
            high, low = halves(contract3(part, inverse, 1, 1))
            high_ref[pl.ds(start, share), :] = high
            low_ref[pl.ds(start, share), :] = low

    out_ref[...] = contract3((high_ref[...], low_ref[...]), halves(frontal_ref[...]), 0, 0)


def first_couplings(index, inverse, frontal, pieces, blocks, done):
    rows, cols = frontal.shape
    share, width = pieces[0].shape
    split = pltpu.VMEM((rows, width), BF16)
    return pl.pallas_call(
        functools.partial(first_coupling_kernel, len(pieces)),
        grid_spec=pltpu.PrefetchScalarGridSpec(
            num_scalar_prefetch=1,
            grid=(done,),
            in_specs=[VMEM, pl.BlockSpec((rows, cols // blocks), lambda b, index: (0, b))]
            + [VMEM] * len(pieces),
            out_specs=(
                pl.BlockSpec((share, width), lambda b, index: (0, 0)),
                VMEM,
                pl.BlockSpec((width, cols // blocks), lambda b, index: (0, b)),
                VMEM,
                VMEM,
            ),
        ),
        out_shape=(
            jax.ShapeDtypeStruct((share, width), F32),
            pltpu.VMEM((share, width), F32),
            jax.ShapeDtypeStruct((width, cols), F32),
            split,
            split,
        ),
        compiler_params=ROOM,
        name="first_couplings",
    )(index, kept(inverse), far(frontal), *[kept(piece) for piece in pieces])


def more_coupling_kernel(high_ref, low_ref, frontal_ref, before_ref, after_ref, out_ref):
    out_ref[...] = contract3((high_ref[...], low_ref[...]), halves(frontal_ref[...]), 0, 0)


def more_couplings(high, low, frontal, before, after, blocks, done):
    rows, cols = frontal.shape
    width = high.shape[1]
    return pl.pallas_call(
        more_coupling_kernel,
        grid=(blocks - done,),
        in_specs=[
            VMEM,
            VMEM,
            pl.BlockSpec((rows, cols // blocks), lambda b: (0, b + done)),
            pl.BlockSpec(memory_space=pl.ANY),
            pl.BlockSpec(memory_space=pl.ANY),
        ],
        out_specs=pl.BlockSpec((width, cols // blocks), lambda b: (0, b + done)),
        out_shape=jax.ShapeDtypeStruct((width, cols), F32),
        input_output_aliases={3: 0},
        compiler_params=ROOM,
        name="more_couplings",
    )(kept(high), kept(low), frontal, before, after)


def node_start(first, core, own_ref, half_refs, coords_ref, top_ref, s_ref, e_ref):
    mid = own_ref.shape[0] // 2
    mine, other = half_refs[0][...], half_refs[1][...]
    top_left = jnp.where(core == 0, mine, other)
    low_right = jnp.where(core == 0, other, mine)
    s_ref[:mid, :mid] = own_ref[:mid, :mid] + top_left[:mid, :]
    s_ref[mid:, mid:] = own_ref[mid:, mid:] + low_right[:mid, :]
    s_ref[: mid // 2, mid:] = own_ref[: mid // 2, mid:] + top_left[mid:, :]
    s_ref[mid // 2 : mid, mid:] = own_ref[mid // 2 : mid, mid:] + low_right[mid:, :]
    s_ref[mid:, :mid] = jnp.zeros((mid, mid), F32)
    carried = contract3(halves(coords_ref[...]), halves(top_ref[...]), 0, 1 if first else 0)
    if carried.shape[1] < e_ref.shape[1]:
        e_ref[...] = jnp.zeros(e_ref.shape, F32)
    e_ref[:, : carried.shape[1]] = carried


def node_kernel(height, rank_ref, core_ref, own_ref, mine_ref, other_ref, coords_ref, top_ref, next_own_ref, next_coords_ref, next_top_ref, next_half_ref, s_ref, e_ref):
    core = core_ref[0]
    node_start(height == 1, core, own_ref, (mine_ref, other_ref), coords_ref, top_ref, s_ref, e_ref)
    masked_factor(s_ref, e_ref, rank_ref[0], next_coords_ref, next_top_ref, next_own_ref)
    pack_half(next_own_ref, next_half_ref, core)


def last_node_kernel(height, rank_ref, core_ref, own_ref, mine_ref, other_ref, coords_ref, top_ref, out_ref, s_ref, e_ref, r_ref, x_ref):
    node_start(height == 1, core_ref[0], own_ref, (mine_ref, other_ref), coords_ref, top_ref, s_ref, e_ref)
    masked_factor(s_ref, e_ref, rank_ref[0], r_ref, x_ref)
    out_ref[...] = x_ref[...].T[: out_ref.shape[0], :]


def node(rank, core, own, mine, other, coords, top, share, height):
    width = own.shape[0]
    padded = -(-share // LANES) * LANES
    square = pltpu.VMEM((width, width), F32)
    scratch = [pltpu.VMEM((width, width), F32), pltpu.VMEM((width, padded), F32)]
    last = height == LEVELS
    if last:
        kernel, out_shape = last_node_kernel, (jax.ShapeDtypeStruct((share, width), F32),)
        scratch += scratch[:2]
    else:
        kernel = node_kernel
        out_shape = (square, square, pltpu.VMEM((width, padded), F32), half_shape(width))
    return pl.pallas_call(
        functools.partial(kernel, height),
        in_specs=[SMEM] * 2 + [VMEM] * 5,
        out_specs=(VMEM,) * len(out_shape),
        out_shape=out_shape,
        scratch_shapes=scratch,
        compiler_params=ROOM,
        name="last_node" if last else "node",
    )(rank, core, *[kept(array) for array in (own, mine, other, coords, top)])


def swapped(block, axis, distance):
    count = lax.axis_size(axis)
    route = [(low, low ^ distance) for low in range(count) if low ^ distance < count]
    return lax.ppermute(block, axis, route)


def body(frontal, sketch, rank_table):
    parts = lax.axis_size("col")
    chips = parts // 2
    share = frontal.shape[0] // parts
    index = lax.axis_index("col").astype(jnp.int32).reshape(1)
    core = index % 2
    ranks = lax.dynamic_slice_in_dim(rank_table, lax.axis_index("row"), 1, 1)

    leaving, *split = partial_samples(index, frontal, (sketch,), parts, 1)
    arriving = swapped(leaving, "col", 1)
    (staying,) = partial_samples(index, frontal, tuple(kept(part) for part in split), parts, 0)
    chip_sum = staying + arriving
    part_of = lambda at: chip_sum[at * share : (at + 1) * share]
    total = part_of(0)
    for other in [swapped(part_of(at), "col", 2 * at) for at in range(1, chips)]:
        total = total + other
    gathered = [total] + [swapped(total, "col", 2 * at) for at in range(1, chips)]
    pieces = []
    for piece in gathered:
        pieces += [piece, swapped(piece, "col", 1)]

    inverse, coords, own, half = leaf_factor(ranks[0], core, pieces)
    mine = swapped(half, "row", 1)
    leaf_share, top, coupling, high, low = first_couplings(index, inverse, frontal, pieces, 4, 1)
    for height in range(1, LEVELS):
        mine, coupling = lax.optimization_barrier((mine, coupling))
        other = swapped(mine, "col", 1)
        own, coords, top, half = node(ranks[height], core, own, mine, other, coords, top, share, height)
        mine = swapped(half, "row", 1 << height)
        if height == 1:
            coupling = more_couplings(high, low, frontal, coupling, half, 4, 1)
    mine, coupling = lax.optimization_barrier((mine, coupling))
    other = swapped(mine, "col", 1)
    (top,) = node(ranks[LEVELS], core, own, mine, other, coords, top, share, LEVELS)
    return (leaf_share, top, coupling)


def solution(mesh):
    return jax.shard_map(
        body,
        mesh=mesh,
        in_specs=(P("row", "col"), P("col", None), P()),
        out_specs=(P(("row", "col"), None), P(("row", "col"), None), P("row", "col")),
        check_vma=False,
    )
```

```python
import functools

import jax
import jax.numpy as jnp
from jax import lax
from jax.experimental import pallas as pl
from jax.experimental.pallas import tpu as pltpu
from jax.sharding import PartitionSpec as P


LEVELS = 2
TILE = 8
GROUP = 16
LANES = 128
F32 = jnp.float32
BF16 = jnp.bfloat16
VMEM = pl.BlockSpec(memory_space=pltpu.VMEM)
SMEM = pl.BlockSpec(memory_space=pltpu.SMEM)
ROOM = pltpu.CompilerParams(vmem_limit_bytes=28 << 20)


def far(array):
    return pltpu.with_memory_space_constraint(array, pltpu.HBM)


def kept(array):
    return pltpu.with_memory_space_constraint(array, pltpu.VMEM)


def contract(left, right, dim_left, dim_right, precision=None):
    return lax.dot_general(
        left, right, (((dim_left,), (dim_right,)), ((), ())), precision=precision, preferred_element_type=F32
    )


def halves(value):
    high = value.astype(BF16)
    return high, (value - high.astype(F32)).astype(BF16)


def contract3(left, right, dim_left, dim_right):
    (lh, ll), (rh, rl) = left, right
    return (
        contract(lh, rh, dim_left, dim_right)
        + contract(lh, rl, dim_left, dim_right)
        + contract(ll, rh, dim_left, dim_right)
    )


def over_lanes(tile, lane):
    return jnp.broadcast_to(tile[:, lane : lane + 1], tile.shape)


def over_rows(tile, row):
    return jnp.broadcast_to(tile[row : row + 1, :], tile.shape)


def along_lanes(tile, index):
    return jnp.take_along_axis(tile, index, axis=1, mode="promise_in_bounds")


def packed_contract3(left, right):
    (lh, ll), (rh, rl) = left, right
    return contract(jnp.concatenate([lh, lh, ll], axis=0), jnp.concatenate([rh, rl, rh], axis=0), 0, 0)


def eliminate(parts, outs, low, rank, update):
    n = parts[0][0].shape[0]
    at = low - parts[0][1]
    own = GROUP // TILE
    count = min(2 * own, (n - low) // TILE)
    sub = lax.broadcasted_iota(jnp.int32, (TILE, LANES), 0)
    lane = lax.broadcasted_iota(jnp.int32, (TILE, LANES), 1)
    span = lambda t: slice(low + TILE * t, low + TILE * (t + 1))
    work = [[ref[span(t), c : c + LANES] for ref, c in parts] for t in range(count)]
    less = update()
    diag = [over_lanes(work[0][0], at + k) for k in range(TILE)]
    for t in range(own):
        left = rank - (low + TILE * t)
        cols = ahead = None
        if t + 1 < own:
            cols = [over_lanes(work[t + 1][0], at + TILE * t + k) for k in range(TILE)]
            ahead = [over_lanes(work[t + 1][0], at + TILE * (t + 1) + k) for k in range(TILE)]
        for k in range(TILE):
            diag[k] = jnp.where((sub < left) & (left > k), diag[k], (sub == k).astype(F32))
        pivots = None
        pivot = over_rows(diag[0], 0)
        for j in range(TILE):
            below = [over_rows(diag[k], j) if k > j else None for k in range(TILE)]
            scale = 1.0 / pivot
            lower = jnp.where(sub > j, diag[j], 0.0)
            pivots = pivot if pivots is None else jnp.where(sub == j, pivot, pivots)
            if j + 1 < TILE:
                pivot = over_rows(diag[j + 1], j + 1) - over_rows(diag[j], j + 1) * below[j + 1] * scale
            for k in range(j + 1, TILE):
                diag[k] = diag[k] - (lower * below[k]) * scale
            scale = jnp.where(left > j, scale, 0.0)
            row = [over_rows(part, j) for part in work[t]]
            scaled = [part * scale for part in row]
            for u in range(t + 1, count):
                ahead_of = at + TILE * u
                if u == t + 1 and cols is not None:
                    column = cols[j]
                    column_scaled = column * scale
                    for k in range(j + 1, TILE):
                        cols[k] = cols[k] - column_scaled * below[k]
                    for k in range(TILE):
                        ahead[k] = ahead[k] - column_scaled * over_rows(column, k)
                else:
                    column = along_lanes(row[ahead_of // LANES], sub + ahead_of % LANES)
                work[u] = [part - column * other for part, other in zip(work[u], scaled)]
            work[t] = [part - lower * other for part, other in zip(work[t], scaled)]
        root = jnp.where(sub < left, lax.rsqrt(pivots), 0.0)
        for part, (ref, c, upper) in zip(work[t], outs):
            part = part * root
            if upper:
                part = jnp.where(lane + c >= sub + (low + TILE * t), part, 0.0)
            ref[span(t), c : c + LANES] = part
        if t + 1 < own:
            diag = ahead
    past = low + GROUP
    for t in range(own, count):
        for q, (ref, c) in enumerate(parts):
            part = work[t][q]
            if less is not None and less[q] is not None and TILE * (t - own) < less[q].shape[0]:
                part = part - less[q][TILE * (t - own) : TILE * (t - own + 1)]
            ref[span(t), c : c + LANES] = part
    if less is not None:
        for q, (ref, c) in enumerate(parts):
            if less[q] is not None:
                begin, end = low + TILE * count, past + less[q].shape[0]
                if begin < end:
                    ref[begin:end, c : c + LANES] = ref[begin:end, c : c + LANES] - less[q][begin - past :]


def masked_factor(s_ref, e_ref, rank, coords_ref, x_ref, own_ref=None, growing=False):
    n = s_ref.shape[0]
    wide = e_ref.shape[1]
    coords_ref[...] = jnp.zeros(coords_ref.shape, F32)
    x_ref[...] = jnp.zeros(x_ref.shape, F32)
    if own_ref is not None:
        own_ref[...] = s_ref[...]
    extent_at = lambda low: min(wide, low // LANES * LANES + LANES) if growing else wide
    for low in range(0, n, GROUP):
        slab = low // LANES * LANES
        s_at = list(range(slab, n, LANES))
        e_at = list(range(0, extent_at(low), LANES))
        parts = [(s_ref, c) for c in s_at] + [(e_ref, c) for c in e_at]
        outs = [(coords_ref, c, True) for c in s_at] + [(x_ref, c, False) for c in e_at]

        def update(low=low, slab=slab, s_at=s_at, e_at=e_at):
            past = low + GROUP
            if low == 0 or past >= n:
                return None
            before = slice(low - GROUP, low)
            panel = halves(coords_ref[before, slab:])
            known = extent_at(low - GROUP)
            right = panel
            if known:
                right = tuple(
                    jnp.concatenate(pair, axis=1) for pair in zip(panel, halves(x_ref[before, :known]))
                )
            left = tuple(part[:, past - slab :] for part in panel)
            cut = slab + LANES - past
            if cut <= 0 or slab + LANES == n:
                product = packed_contract3(left, right)
                less = [product[:, c - slab : c - slab + LANES] for c in s_at]
            else:
                upper = packed_contract3(tuple(part[:, :cut] for part in left), tuple(part[:, :LANES] for part in right))
                product = packed_contract3(left, tuple(part[:, LANES:] for part in right))
                product = jnp.concatenate([jnp.zeros((product.shape[0], LANES), F32), product], axis=1)
                less = [upper] + [product[:, c - slab : c - slab + LANES] for c in s_at[1:]]
            return less + [
                product[:, n - slab + c : n - slab + c + LANES] if c < known else None for c in e_at
            ]

        pl.when(rank > low)(functools.partial(eliminate, parts, outs, low, rank, update))
    if own_ref is not None:

        @pl.when(rank < n)
        def _():
            rows = lax.broadcasted_iota(jnp.int32, (n, n), 0)
            cols = lax.broadcasted_iota(jnp.int32, (n, n), 1)
            panel = halves(coords_ref[...])
            outside = (rows < rank) | (cols < rank)
            own_ref[...] = jnp.where(outside, own_ref[...], contract3(panel, panel, 0, 0))


def first_samples_kernel(count, index_ref, *refs):
    frontal_refs, (sketch_ref, out_ref, high_ref, low_ref) = refs[:count], refs[count:]

    @pl.when(pl.program_id(0) == 0)
    def _():
        high_ref[...], low_ref[...] = halves(sketch_ref[...])

    samples_kernel(count, index_ref, *frontal_refs, high_ref, low_ref, out_ref)


def samples_kernel(count, index_ref, *refs):
    frontal_refs, (high_ref, low_ref, out_ref) = refs[:count], refs[count:]
    rows = halves(jnp.concatenate([ref[...] for ref in frontal_refs], axis=0))
    size = rows[0].shape[0]
    start = pl.multiple_of(pl.program_id(0) * size, size)
    out_ref[pl.ds(start, size), :] = contract3(rows, (high_ref[...], low_ref[...]), 1, 0)


def partial_samples(index, frontal, sketch, parts, offset, blocks=2):
    share, inner = frontal.shape[0] // parts, frontal.shape[1]
    width = sketch[0].shape[1]
    count = parts // 2 // blocks
    out_shape = (pltpu.VMEM((parts // 2 * share, width), F32),)
    first = len(sketch) == 1
    if first:
        out_shape += (pltpu.VMEM((inner, width), BF16),) * 2

    def rows_of(d):
        return pl.BlockSpec((share, inner), lambda k, index: (index[0] ^ (2 * (count * k + d) + offset), 0))

    return pl.pallas_call(
        functools.partial(first_samples_kernel if first else samples_kernel, count),
        grid_spec=pltpu.PrefetchScalarGridSpec(
            num_scalar_prefetch=1,
            grid=(blocks,),
            in_specs=[rows_of(d) for d in range(count)]
            + ([pl.BlockSpec((inner, width), lambda k, index: (0, 0))] if first else [VMEM, VMEM]),
            out_specs=(VMEM,) * len(out_shape),
        ),
        out_shape=out_shape,
        compiler_params=ROOM,
        name="first_samples" if first else "more_samples",
    )(index, *[far(frontal)] * count, *(sketch if not first else map(far, sketch)))


def unit_matrix(shape):
    rows = lax.broadcasted_iota(jnp.int32, shape, 0)
    cols = lax.broadcasted_iota(jnp.int32, shape, 1)
    return (rows == cols).astype(F32)


def pack_half(square_ref, half_ref, core):
    mid = square_ref.shape[0] // 2
    first = core == 0
    half_ref[:mid, :] = jnp.where(first, square_ref[:mid, :mid], square_ref[mid:, mid:])
    half_ref[mid:, :] = jnp.where(first, square_ref[: mid // 2, mid:], square_ref[mid // 2 : mid, mid:])


def leaf_kernel(rank_ref, core_ref, *refs):
    pieces, (p_ref, coords_ref, own_ref, half_ref, s_ref, e_ref) = refs[:-6], refs[-6:]
    e_ref[...] = unit_matrix(e_ref.shape)
    samples = halves(jnp.concatenate([piece[...] for piece in pieces], axis=0))
    s_ref[...] = contract3(samples, samples, 0, 0)
    masked_factor(s_ref, e_ref, rank_ref[0], coords_ref, p_ref, own_ref, growing=True)
    pack_half(own_ref, half_ref, core_ref[0])


def half_shape(width):
    return pltpu.VMEM((width * 3 // 4, width // 2), F32)


def leaf_factor(rank, core, pieces):
    width = pieces[0].shape[1]
    square = pltpu.VMEM((width, width), F32)
    return pl.pallas_call(
        leaf_kernel,
        in_specs=[SMEM] * 2 + [VMEM] * len(pieces),
        out_specs=(VMEM,) * 4,
        out_shape=(square,) * 3 + (half_shape(width),),
        scratch_shapes=[pltpu.VMEM((width, width), F32)] * 2,
        compiler_params=ROOM,
        name="leaf_factor",
    )(rank, core, *[kept(piece) for piece in pieces])


def leaf_basis_kernel(count, index_ref, p_ref, *refs):
    pieces, (share_ref, near_ref, high_ref, low_ref) = refs[:count], refs[count:]
    share = pieces[0].shape[0]
    inverse = halves(p_ref[...])
    for at, piece in enumerate(pieces):
        basis = contract3(halves(piece[...]), inverse, 1, 1)
        if at == 0:
            near_ref[...] = basis
            share_ref[...] = basis
        start = pl.multiple_of((index_ref[0] ^ at) * share, share)
        high, low = halves(basis)
        high_ref[pl.ds(start, share), :] = high
        low_ref[pl.ds(start, share), :] = low


def leaf_basis(index, inverse, pieces):
    share, width = pieces[0].shape
    split = pltpu.VMEM((share * len(pieces), width), BF16)
    return pl.pallas_call(
        functools.partial(leaf_basis_kernel, len(pieces)),
        in_specs=[SMEM, VMEM] + [VMEM] * len(pieces),
        out_specs=(VMEM,) * 4,
        out_shape=(jax.ShapeDtypeStruct((share, width), F32), pltpu.VMEM((share, width), F32), split, split),
        compiler_params=ROOM,
        name="leaf_basis",
    )(index, kept(inverse), *[kept(piece) for piece in pieces])


def coupling_kernel(high_ref, low_ref, frontal_ref, after_ref, out_ref):
    out_ref[...] = contract3((high_ref[...], low_ref[...]), halves(frontal_ref[...]), 0, 0)


def couplings(high, low, frontal, after, blocks=2):
    rows, cols = frontal.shape
    width = high.shape[1]
    return pl.pallas_call(
        coupling_kernel,
        grid=(blocks,),
        in_specs=[
            VMEM,
            VMEM,
            pl.BlockSpec((rows, cols // blocks), lambda b: (0, b)),
            pl.BlockSpec(memory_space=pl.ANY),
        ],
        out_specs=pl.BlockSpec((width, cols // blocks), lambda b: (0, b)),
        out_shape=jax.ShapeDtypeStruct((width, cols), F32),
        compiler_params=ROOM,
        name="couplings",
    )(kept(high), kept(low), far(frontal), after)


def node_start(first, core, own_ref, half_refs, coords_ref, top_ref, s_ref, e_ref):
    mid = own_ref.shape[0] // 2
    mine, other = half_refs[0][...], half_refs[1][...]
    top_left = jnp.where(core == 0, mine, other)
    low_right = jnp.where(core == 0, other, mine)
    s_ref[:mid, :mid] = own_ref[:mid, :mid] + top_left[:mid, :]
    s_ref[mid:, mid:] = own_ref[mid:, mid:] + low_right[:mid, :]
    s_ref[: mid // 2, mid:] = own_ref[: mid // 2, mid:] + top_left[mid:, :]
    s_ref[mid // 2 : mid, mid:] = own_ref[mid // 2 : mid, mid:] + low_right[mid:, :]
    s_ref[mid:, :mid] = jnp.zeros((mid, mid), F32)
    carried = contract3(halves(coords_ref[...]), halves(top_ref[...]), 0, 1 if first else 0)
    if carried.shape[1] < e_ref.shape[1]:
        e_ref[...] = jnp.zeros(e_ref.shape, F32)
    e_ref[:, : carried.shape[1]] = carried


def node_kernel(height, rank_ref, core_ref, own_ref, mine_ref, other_ref, coords_ref, top_ref, next_own_ref, next_coords_ref, next_top_ref, next_half_ref, s_ref, e_ref):
    core = core_ref[0]
    node_start(height == 1, core, own_ref, (mine_ref, other_ref), coords_ref, top_ref, s_ref, e_ref)
    masked_factor(s_ref, e_ref, rank_ref[0], next_coords_ref, next_top_ref, next_own_ref)
    pack_half(next_own_ref, next_half_ref, core)


def last_node_kernel(height, rank_ref, core_ref, own_ref, mine_ref, other_ref, coords_ref, top_ref, out_ref, s_ref, e_ref, r_ref, x_ref):
    node_start(height == 1, core_ref[0], own_ref, (mine_ref, other_ref), coords_ref, top_ref, s_ref, e_ref)
    masked_factor(s_ref, e_ref, rank_ref[0], r_ref, x_ref)
    out_ref[...] = x_ref[...].T[: out_ref.shape[0], :]


def node(rank, core, own, mine, other, coords, top, share, height):
    width = own.shape[0]
    padded = -(-share // LANES) * LANES
    square = pltpu.VMEM((width, width), F32)
    scratch = [pltpu.VMEM((width, width), F32), pltpu.VMEM((width, padded), F32)]
    last = height == LEVELS
    if last:
        kernel, out_shape = last_node_kernel, (jax.ShapeDtypeStruct((share, width), F32),)
        scratch += scratch[:2]
    else:
        kernel = node_kernel
        out_shape = (square, square, pltpu.VMEM((width, padded), F32), half_shape(width))
    return pl.pallas_call(
        functools.partial(kernel, height),
        in_specs=[SMEM] * 2 + [VMEM] * 5,
        out_specs=(VMEM,) * len(out_shape),
        out_shape=out_shape,
        scratch_shapes=scratch,
        compiler_params=ROOM,
        name="last_node" if last else "node",
    )(rank, core, *[kept(array) for array in (own, mine, other, coords, top)])


def swapped(block, axis, distance):
    count = lax.axis_size(axis)
    route = [(low, low ^ distance) for low in range(count) if low ^ distance < count]
    return lax.ppermute(block, axis, route)


def body(frontal, sketch, rank_table):
    parts = lax.axis_size("col")
    chips = parts // 2
    share = frontal.shape[0] // parts
    index = lax.axis_index("col").astype(jnp.int32).reshape(1)
    core = index % 2
    ranks = lax.dynamic_slice_in_dim(rank_table, lax.axis_index("row"), 1, 1)

    leaving, *split = partial_samples(index, frontal, (sketch,), parts, 1)
    arriving = swapped(leaving, "col", 1)
    (staying,) = partial_samples(index, frontal, tuple(kept(part) for part in split), parts, 0)
    chip_sum = staying + arriving
    part_of = lambda at: chip_sum[at * share : (at + 1) * share]
    total = part_of(0)
    for other in [swapped(part_of(at), "col", 2 * at) for at in range(1, chips)]:
        total = total + other
    gathered = [total] + [swapped(total, "col", 2 * at) for at in range(1, chips)]
    pieces = []
    for piece in gathered:
        pieces += [piece, swapped(piece, "col", 1)]

    inverse, coords, own, half = leaf_factor(ranks[0], core, pieces)
    mine = swapped(half, "row", 1)
    leaf_share, top, high, low = leaf_basis(index, inverse, pieces)
    for height in range(1, LEVELS):
        mine, top = lax.optimization_barrier((mine, top))
        other = swapped(mine, "col", 1)
        own, coords, top, half = node(ranks[height], core, own, mine, other, coords, top, share, height)
        mine = swapped(half, "row", 1 << height)
        if height == 1:
            coupling = couplings(high, low, frontal, half)
    mine, coupling = lax.optimization_barrier((mine, coupling))
    other = swapped(mine, "col", 1)
    (top,) = node(ranks[LEVELS], core, own, mine, other, coords, top, share, LEVELS)
    return (leaf_share, top, coupling)


def solution(mesh):
    return jax.shard_map(
        body,
        mesh=mesh,
        in_specs=(P("row", "col"), P("col", None), P()),
        out_specs=(P(("row", "col"), None), P(("row", "col"), None), P("row", "col")),
        check_vma=False,
    )
```
